128 devices in a mesh: lat: 8 (over x, core), lon: 16 (over z, y).
Axes of the slice: x: 4, y: 4, z: 4, core: 2. Of those that a mesh axis runs over, the one named last changes fastest.
Arguments:
- latent_field: float32 [32, 8, 128, 2048], P(None, None, 'lat', 'lon'), may hold values from -6 to 6
- east_courant: float32 [8, 128, 2048], P(None, 'lat', 'lon'), may hold values from -0.45 to 0.45
- north_courant: float32 [8, 128, 2048], P(None, 'lat', 'lon'), may hold values from -0.45 to 0.45
- mixing: float32 [7, 128, 2048], P(None, 'lat', 'lon'), may hold values from 0.2 to 5
- sunlit: int32 [8, 128], P('lat', 'lon'), may hold values from 0 to 1, as said below
- decode_w: bfloat16 [224, 32], replicated, may hold values from -1 to 1
- react_a: bfloat16 [256, 224], replicated, may hold values from -0.375 to 0.375
- react_b: bfloat16 [256, 224], replicated, may hold values from -0.375 to 0.375
- stoich: bfloat16 [224, 256], replicated, may hold values from -0.375 to 0.375
- encode_w: bfloat16 [32, 224], replicated, may hold values from -0.375 to 0.375
- rate_const: float32 [256], replicated, may hold values from 0.05 to 0.5
Outputs:
- advanced: float32 [32, 8, 128, 2048], P(None, None, 'lat', 'lon')
The draws below stay inside these ranges and needn't reach their ends.
Inputs may be any that keep to these rules, and one draw needn't show every extreme that they name: In each row of blocks the sunlit blocks form one run, periodic in longitude, of 32 to 96 blocks.
All inputs are finite; a program needn't handle non-finite values.
Results may differ from the reference program's by a relative error of at most 0.0035.
Values may be sent and summed in bfloat16 or wider, within the bound.
A program may use at most 128 MiB of HBM per device.

```python
import math
import jax
import jax.numpy as jnp
from jax import lax

S = 32
NSP = 224
NR = 256
LEV = 8
BLOCK = 16
SUBSTEPS = 2
STEPS = 2
NLAT = 128
NLON = 2048
BLOCK_ROWS = 8
BLOCK_COLS = 128


def draw_sunlit(key, part):
    centre_key, width_key = jax.random.split(key)
    centres = jax.random.randint(centre_key, (BLOCK_ROWS, 1), 0, BLOCK_COLS)
    widths = jax.random.randint(width_key, (BLOCK_ROWS, 1), BLOCK_COLS // 4, 3 * BLOCK_COLS // 4 + 1)
    columns = jnp.arange(BLOCK_COLS)[None, :]
    return ((columns - centres) % BLOCK_COLS < widths).astype(jnp.int32)


def block_levels(key, shape, cuts, smallest, top_value):
    gain, own = 1.0, jax.random.fold_in(key, 6)
    for axis_at, blocks in cuts:
        draws = jnp.exp(jax.random.uniform(jax.random.fold_in(own, axis_at), (blocks,), jnp.float32, smallest / len(cuts), top_value / len(cuts)))
        gain = gain * jnp.repeat(draws, shape[axis_at] // blocks).reshape([-1 if axis == axis_at else 1 for axis in range(len(shape))])
    return gain


def noise(rng, dims, spread, reach, cuts=(), kind=jnp.bfloat16):
    array = jax.random.normal(rng, dims, jnp.float32) * spread
    if len(cuts) > 0:
        array = block_levels(rng, dims, cuts, -0.22, 0.18) * array
    return jnp.clip(array, min=-reach, max=reach).astype(kind)


def setup_inputs(seed: int = 0) -> dict:
    streams_of = jax.random.split(jax.random.key(seed), 12)
    latent_field = noise(streams_of[0], (S, LEV, NLAT, NLON), 1.0, 6.0, ((2, 8), (3, 16)), jnp.float32)
    east_courant = jnp.clip(jax.random.uniform(streams_of[1], (LEV, NLAT, NLON), jnp.float32, -0.45, 0.45) * block_levels(streams_of[1], (LEV, NLAT, NLON), ((1, 8), (2, 16)), -0.4, 0.0), -0.45, 0.45)
    north_courant = jnp.clip(jax.random.uniform(streams_of[2], (LEV, NLAT, NLON), jnp.float32, -0.45, 0.45) * block_levels(streams_of[2], (LEV, NLAT, NLON), ((1, 8), (2, 16)), -0.4, 0.0), -0.45, 0.45)
    mixing = jnp.clip(jnp.exp(math.log(5.0) - 3.218876 * jax.random.uniform(streams_of[3], (LEV - 1, NLAT, NLON), jnp.float32) ** block_levels(streams_of[3], (LEV - 1, NLAT, NLON), ((1, 8), (2, 16)), -0.2, 0.2)), 0.2, 5.0)
    sunlit = draw_sunlit(jax.random.fold_in(streams_of[11], 71), 0)
    decode_w = noise(streams_of[5], (NSP, S), S ** -0.5, 1.0)
    react_a = noise(streams_of[6], (NR, NSP), NSP ** -0.5, 0.375)
    react_b = noise(streams_of[7], (NR, NSP), NSP ** -0.5, 0.375)
    stoich = noise(streams_of[8], (NSP, NR), NR ** -0.5, 0.375)
    encode_w = noise(streams_of[9], (S, NSP), NSP ** -0.5, 0.375)
    rate_const = jnp.clip(jnp.exp(jax.random.uniform(streams_of[10], (NR,), jnp.float32, math.log(0.05), math.log(0.5))), 0.05, 0.5)
    return dict(latent_field=latent_field, east_courant=east_courant, north_courant=north_courant, mixing=mixing, sunlit=sunlit, decode_w=decode_w, react_a=react_a, react_b=react_b, stoich=stoich, encode_w=encode_w, rate_const=rate_const)


def advect(latent_field, east_courant, north_courant):
    lat_cells = latent_field.shape[2]
    east_speed = east_courant[None]
    north_speed = north_courant[None]
    east_face = jnp.maximum(east_speed, 0.0) * latent_field + jnp.minimum(jnp.roll(east_speed, -1, 3), 0.0) * jnp.roll(latent_field, -1, 3)
    north_face = jnp.maximum(north_speed, 0.0) * latent_field + jnp.minimum(jnp.roll(north_speed, -1, 2), 0.0) * jnp.roll(latent_field, -1, 2)
    north_open = jnp.arange(lat_cells) < lat_cells - 1
    north_face = jnp.where(north_open[:, None], north_face, 0.0)
    return latent_field - (east_face - jnp.roll(east_face, 1, 3)) - (north_face - jnp.roll(north_face, 1, 2))


def diffuse(tracers, mixing):
    n_levels = tracers.shape[1]
    sweep_upper = []
    sweep_right = []
    for level_index in range(n_levels):
        below_mix = mixing[level_index - 1][None] if level_index > 0 else 0.0
        above_mix = mixing[level_index][None] if level_index < n_levels - 1 else 0.0
        diagonal = 1.0 + below_mix + above_mix
        if level_index > 0:
            pivot_value = diagonal + below_mix * sweep_upper[-1]
            right_side = tracers[:, level_index] + below_mix * sweep_right[-1]
        else:
            pivot_value = diagonal
            right_side = tracers[:, 0]
        sweep_upper.append(-above_mix / pivot_value)
        sweep_right.append(right_side / pivot_value)
    solved = [sweep_right[-1]]
    for level_index in range(n_levels - 2, -1, -1):
        solved.insert(0, sweep_right[level_index] - sweep_upper[level_index] * solved[0])
    return jnp.stack(solved, 1)


def chemistry(latent_in, species_in, decode_w, react_a, react_b, stoich, encode_w, rate_const):
    current = latent_in.astype(jnp.float32)
    summed = jnp.zeros(current.shape, jnp.float32)
    species = species_in
    for substep in range(SUBSTEPS):
        if substep > 0:
            species = jnp.dot(decode_w, current.astype(jnp.bfloat16), preferred_element_type=jnp.float32).astype(jnp.bfloat16)
        react_first = jnp.dot(react_a, species, preferred_element_type=jnp.float32)
        react_second = jnp.dot(react_b, species, preferred_element_type=jnp.float32)
        rate_values = (rate_const[:, None] * react_first * react_second).astype(jnp.bfloat16)
        tendency = jnp.dot(stoich, rate_values, preferred_element_type=jnp.float32).astype(jnp.bfloat16)
        increment = jnp.dot(encode_w, tendency, preferred_element_type=jnp.float32).astype(jnp.bfloat16)
        increment = lax.optimization_barrier(increment).astype(jnp.float32)
        summed = summed + increment
        current = current + increment
    return summed.astype(jnp.bfloat16)


def reference(latent_field, east_courant, north_courant, mixing, sunlit, decode_w, react_a, react_b, stoich, encode_w, rate_const):
    n_species, n_levels, lat_cells, lon_cells = latent_field.shape
    block_rows = lat_cells // BLOCK
    block_cols = lon_cells // BLOCK
    sun_flags = sunlit.reshape(-1)

    def react_block(pieces):
        block_data, sun_flag = pieces

        def lit_branch(values):
            latent_in = values.astype(jnp.bfloat16)
            species = jnp.dot(decode_w, latent_in, preferred_element_type=jnp.float32).astype(jnp.bfloat16)
            return chemistry(latent_in, species, decode_w, react_a, react_b, stoich, encode_w, rate_const)

        def dark_branch(values):
            return jnp.zeros(values.shape, jnp.bfloat16)

        return lax.cond(sun_flag > 0, lit_branch, dark_branch, block_data)

    for step_index in range(STEPS):
        tracers = diffuse(advect(latent_field, east_courant, north_courant), mixing)
        blocks = tracers.reshape(n_species, n_levels, block_rows, BLOCK, block_cols, BLOCK).transpose(2, 4, 0, 1, 3, 5).reshape(block_rows * block_cols, n_species, n_levels * BLOCK * BLOCK)
        increments = lax.map(react_block, (blocks, sun_flags))
        blocks = blocks + increments.astype(jnp.float32)
        latent_field = blocks.reshape(block_rows, block_cols, n_species, n_levels, BLOCK, BLOCK).transpose(2, 3, 0, 4, 1, 5).reshape(n_species, n_levels, lat_cells, lon_cells)
    return latent_field
```

```python
import jax
import jax.numpy as jnp
from jax import lax
from jax.experimental import pallas as pl
from jax.experimental.pallas import tpu as pltpu
from jax.sharding import PartitionSpec as P

S = 32
LEV = 8
ROWS = 16
COLS = 128
BLOCK = 16
JOBS = ROWS // 2
FIRST = 11
F32 = jnp.float32
BF16 = jnp.bfloat16
MESH = pl.DeviceIdType.MESH


def dot(a, b):
    return jnp.dot(a, b, preferred_element_type=F32)


def kernel(
    x_hbm, ce_hbm, cn_hbm, mix_hbm, sun_hbm, dec_hbm, ra_hbm, rb_hbm, st_hbm, en_hbm, rc_hbm,
    out_hbm,
    X, da, db, w0, ep, em, epm, nps, nms, lower, upper, inv,
    ce, cn, mix, sun, mask, dec, ra, rb, st, en, rc, aw, bw, ew,
    packed, west, east, halo, to_north, to_south,
    row_sem, small_sem, weight_sem, out_sem, send_sem, recv_sem,
):
    n_lat, n_lon = lax.axis_size("lat"), lax.axis_size("lon")
    lat, lon = lax.axis_index("lat"), lax.axis_index("lon")
    north, south = {"lat": lax.rem(lat + 1, n_lat)}, {"lat": lax.rem(lat + n_lat - 1, n_lat)}
    right, left = {"lon": lax.rem(lon + 1, n_lon)}, {"lon": lax.rem(lon + n_lon - 1, n_lon)}

    barrier = pltpu.get_barrier_semaphore()
    for neighbour in (north, south, right, left):
        pl.semaphore_signal(barrier, inc=1, device_id=neighbour, device_id_type=MESH)

    small = [
        pltpu.make_async_copy(a, b, small_sem.at[i])
        for i, (a, b) in enumerate(((ce_hbm, ce), (cn_hbm, cn), (mix_hbm, mix), (sun_hbm, sun)))
    ]
    weights = [
        pltpu.make_async_copy(a, b, weight_sem.at[i])
        for i, (a, b) in enumerate(
            ((dec_hbm, dec), (ra_hbm, ra), (rb_hbm, rb), (st_hbm, st), (en_hbm, en), (rc_hbm, rc))
        )
    ]
    for copy in small:
        copy.start()

    def load_rows(i, carry):
        r, l = lax.rem(i // LEV + ROWS - 1, ROWS), lax.rem(i, LEV)
        pltpu.make_async_copy(x_hbm.at[:, l, r, :], X.at[0, r + 1, l], row_sem.at[r]).start()
        return carry

    lax.fori_loop(0, ROWS * LEV, load_rows, 0)
    for copy in weights:
        copy.start()

    def wait_row(r):
        pltpu.make_async_copy(da.at[0], X.at[0, r + 1], row_sem.at[r]).wait()

    for copy in small:
        copy.wait()
    lane = lax.broadcasted_iota(jnp.int32, (ROWS, COLS), 1)
    row = lax.broadcasted_iota(jnp.int32, (ROWS, COLS), 0)
    grid_row = row + lat * ROWS
    open_north, open_south = grid_row < n_lat * ROWS - 1, grid_row > 0
    for l in range(LEV):
        c, n = ce[l], cn[l]
        e_plus, e_minus = jnp.maximum(c, 0.0), jnp.minimum(c, 0.0)
        n_plus = jnp.where(open_north, jnp.maximum(n, 0.0), 0.0)
        n_minus = jnp.where(open_south, jnp.minimum(n, 0.0), 0.0)
        ep[l], em[l] = e_plus, e_minus
        epm[l] = jnp.where(lane == COLS - 1, e_plus, e_minus)
        w0[l] = 1.0 - (e_plus - e_minus) - (n_plus - n_minus)
        nps[l] = jnp.where(row == 0, 1.0, pltpu.roll(n_plus, 1, 0))
        nms[l] = jnp.where(row == ROWS - 1, 1.0, pltpu.roll(n_minus, ROWS - 1, 0))
        if l == 0:
            south_factor = n_minus[0:1]
            north_factor = n_plus[ROWS - 1 :]
            factors = [(north_factor, south_factor)]
        else:
            factors.append((n_plus[ROWS - 1 :], n_minus[0:1]))

    wait_row(ROWS - 1)
    wait_row(0)
    for l in range(LEV):
        to_north[0, l] = X[0, ROWS, l] * factors[l][0]
        to_south[0, l] = X[0, 1, l] * factors[l][1]
    pl.semaphore_wait(barrier, 4)

    def edge_copies(step):
        return (
            pltpu.make_async_remote_copy(
                src_ref=to_north.at[step], dst_ref=X.at[step, 0],
                send_sem=send_sem.at[step, 0], recv_sem=recv_sem.at[step, 0],
                device_id=north, device_id_type=MESH,
            ),
            pltpu.make_async_remote_copy(
                src_ref=to_south.at[step], dst_ref=X.at[step, ROWS + 1],
                send_sem=send_sem.at[step, 1], recv_sem=recv_sem.at[step, 1],
                device_id=south, device_id_type=MESH,
            ),
        )

    def side_copies(step, group):
        return (
            pltpu.make_async_remote_copy(
                src_ref=packed.at[step, group], dst_ref=west.at[step, group],
                send_sem=send_sem.at[step, 2 + 2 * group], recv_sem=recv_sem.at[step, 2 + 2 * group],
                device_id=right, device_id_type=MESH,
            ),
            pltpu.make_async_remote_copy(
                src_ref=packed.at[step, group], dst_ref=east.at[step, group],
                send_sem=send_sem.at[step, 3 + 2 * group], recv_sem=recv_sem.at[step, 3 + 2 * group],
                device_id=left, device_id_type=MESH,
            ),
        )

    for copy in edge_copies(0):
        copy.start()

    wide_lane = lax.broadcasted_iota(jnp.int32, (S, COLS), 1)

    def place(r):
        at = lax.rem(r + ROWS - FIRST, ROWS)
        return at // LEV, lax.rem(at, LEV)

    def pack_row(values, r, slot_step):
        group, slot = place(r)
        line = jnp.zeros((S, COLS), F32)
        for l in range(LEV):
            z = values[l] * epm[l, pl.ds(r, 1), :]
            line = jnp.where(wide_lane // 2 == l, pltpu.roll(z, 2 * l + 1, 1), line)
        line = pltpu.roll(line, 16 * slot, 1)
        packed[slot_step, group] = jnp.where(
            wide_lane // 16 == slot, line, packed[slot_step, group]
        )

    packed[...] = jnp.zeros_like(packed)

    def first_pack(i, carry):
        r = lax.rem(i + FIRST, ROWS)

        @pl.when((r > 0) & (r < ROWS - 1))
        def _():
            wait_row(r)

        pack_row([X[0, r + 1, l] for l in range(LEV)], r, 0)
        return carry

    for group in range(2):
        lax.fori_loop(group * 8, group * 8 + 8, first_pack, 0)
        for copy in side_copies(0, group):
            copy.start()

    pivot_upper = None
    for l in range(LEV):
        below = mix[l - 1] if l > 0 else None
        above = mix[l] if l < LEV - 1 else None
        pivot = 1.0
        if below is not None:
            pivot = pivot + below
        if above is not None:
            pivot = pivot + above
        if below is not None:
            pivot = pivot - below * pivot_upper
            lower[l] = below
        recip = 1.0 / pivot
        inv[l] = recip
        if above is not None:
            pivot_upper = above * recip
            upper[l] = pivot_upper
    block = lax.broadcasted_iota(jnp.int32, (1, COLS), 1) // BLOCK
    lit = jnp.zeros((1, COLS), jnp.int32)
    for b in range(COLS // BLOCK):
        lit = jnp.where(block == b, sun[0:1, b : b + 1], lit)
    mask[...] = lit
    for copy in weights:
        copy.wait()
    aw[...] = dot(ra[...], dec[...]).astype(BF16)
    bw[...] = dot(rb[...], dec[...]).astype(BF16)
    ew[...] = (dot(en[...], st[...]) * rc[...]).astype(BF16)

    def unpack(step, group):
        halo[step, group] = jnp.where(
            lax.rem(wide_lane, 2) == 0,
            pltpu.roll(east[step, group], COLS - 1, 1),
            pltpu.roll(west[step, group], 1, 1),
        )

    def transport(job, dest):
        step, turn = job // JOBS, lax.rem(job, JOBS)
        for k in range(2):
            r = lax.rem(2 * turn + FIRST + 2 * step + k, ROWS)
            group, slot = place(r)
            line = pltpu.roll(halo[step, group], lax.rem(COLS - 16 * slot, COLS), 1)
            solved = []
            for l in range(LEV):
                at = lambda ref: ref[l, pl.ds(r, 1), :]
                q = X[step, r + 1, l]
                side = pltpu.roll(line, COLS - (2 * l + 1), 1)
                from_west = jnp.where(wide_lane == 0, side, pltpu.roll(q * at(ep), 1, 1))
                from_east = jnp.where(
                    wide_lane == COLS - 1, side, pltpu.roll(q * at(em), COLS - 1, 1)
                )
                value = (
                    q * at(w0)
                    + (from_west - from_east)
                    + (X[step, r, l] * at(nps) - X[step, r + 2, l] * at(nms))
                )
                if l > 0:
                    value = value + at(lower) * solved[-1]
                solved.append(value * at(inv))
            value = solved[-1]
            dest[k, LEV - 1] = value
            for l in range(LEV - 2, -1, -1):
                value = solved[l] + upper[l, pl.ds(r, 1), :] * value
                dest[k, l] = value

    def chemistry(job, source):
        step, turn = job // JOBS, lax.rem(job, JOBS)
        current = jnp.concatenate([source[k, l] for k in range(2) for l in range(LEV)], axis=1)
        summed = None
        for substep in range(2):
            lines = current.astype(BF16)
            rates = (dot(aw[...], lines) * dot(bw[...], lines)).astype(BF16)
            change = dot(ew[...], rates)
            summed = change if summed is None else summed + change
            current = current + change
        lit_lanes = jnp.broadcast_to(mask[...], (S, COLS)) > 0
        for k in range(2):
            r = lax.rem(2 * turn + FIRST + 2 * step + k, ROWS)
            values = []
            for l in range(LEV):
                at = (k * LEV + l) * COLS
                value = source[k, l] + jnp.where(lit_lanes, summed[:, at : at + COLS], 0.0)
                X[step + 1, r + 1, l] = value
                values.append(value)
            pack_row(values, r, step + 1)

    def after(job):
        @pl.when(job == 2)
        def _():
            for l in range(LEV):
                to_north[1, l] = X[1, ROWS, l] * jnp.where(
                    lat < n_lat - 1, jnp.maximum(cn[l, ROWS - 1 :, :], 0.0), 0.0
                )
                to_south[1, l] = X[1, 1, l] * jnp.where(
                    lat > 0, jnp.minimum(cn[l, 0:1, :], 0.0), 0.0
                )
            for copy in edge_copies(1):
                copy.start()

        for group in range(2):

            @pl.when(job == 3 + 4 * group)
            def _():
                for copy in side_copies(1, group):
                    copy.start()

        @pl.when(job >= JOBS)
        def _():
            def store(i, carry):
                r = lax.rem(2 * (job - JOBS) + FIRST + 2 + i // LEV, ROWS)
                l = lax.rem(i, LEV)
                pltpu.make_async_copy(X.at[2, r + 1, l], out_hbm.at[:, l, r, :], out_sem).start()
                return carry

            lax.fori_loop(0, 2 * LEV, store, 0)

    def before(job):
        @pl.when(job == JOBS - 1)
        def _():
            for copy in edge_copies(1):
                copy.wait()
            for copy in side_copies(1, 0):
                copy.wait()
            unpack(1, 0)

        @pl.when(job == JOBS + 2)
        def _():
            for copy in side_copies(1, 1):
                copy.wait()
            unpack(1, 1)

    for copy in edge_copies(0):
        copy.wait()
    for group in range(2):
        for copy in side_copies(0, group):
            copy.wait()
        unpack(0, group)
    transport(0, da)

    def pair(i, carry):
        for k, (here, there) in enumerate(((da, db), (db, da))):
            job = 2 * i + k
            before(job)
            transport(jnp.minimum(job + 1, 2 * JOBS - 1), there)
            chemistry(job, here)
            after(job)
        return carry

    lax.fori_loop(0, JOBS, pair, 0)
    pltpu.make_async_copy(X.at[0, 1 : ROWS + 1], X.at[2, 1 : ROWS + 1], out_sem).wait()


def on_device(latent_field, east_courant, north_courant, mixing, sunlit, decode_w, react_a, react_b, stoich, encode_w, rate_const):
    coefficient = pltpu.VMEM((LEV, ROWS, COLS), F32)
    tile = pltpu.VMEM((2, LEV, S, COLS), F32)
    n_species, n_reactions = stoich.shape
    return pl.pallas_call(
        kernel,
        name="split_steps",
        out_shape=jax.ShapeDtypeStruct(latent_field.shape, F32),
        in_specs=[pl.BlockSpec(memory_space=pl.ANY)] * 11,
        out_specs=pl.BlockSpec(memory_space=pl.ANY),
        scratch_shapes=[
            pltpu.VMEM((3, ROWS + 2, LEV, S, COLS), F32), tile, tile,
            coefficient, coefficient, coefficient, coefficient, coefficient, coefficient,
            coefficient, coefficient, coefficient,
            coefficient, coefficient, pltpu.VMEM((LEV - 1, ROWS, COLS), F32),
            pltpu.VMEM((1, COLS // BLOCK), jnp.int32), pltpu.VMEM((1, COLS), jnp.int32),
            pltpu.VMEM((n_species, S), BF16),
            pltpu.VMEM((n_reactions, n_species), BF16), pltpu.VMEM((n_reactions, n_species), BF16),
            pltpu.VMEM((n_species, n_reactions), BF16), pltpu.VMEM((S, n_species), BF16),
            pltpu.VMEM((1, n_reactions), F32),
            pltpu.VMEM((n_reactions, S), BF16), pltpu.VMEM((n_reactions, S), BF16),
            pltpu.VMEM((S, n_reactions), BF16),
            pltpu.VMEM((3, 2, S, COLS), F32), pltpu.VMEM((2, 2, S, COLS), F32),
            pltpu.VMEM((2, 2, S, COLS), F32), pltpu.VMEM((2, 2, S, COLS), F32),
            pltpu.VMEM((2, LEV, S, COLS), F32), pltpu.VMEM((2, LEV, S, COLS), F32),
            pltpu.SemaphoreType.DMA((ROWS,)), pltpu.SemaphoreType.DMA((4,)),
            pltpu.SemaphoreType.DMA((6,)), pltpu.SemaphoreType.DMA,
            pltpu.SemaphoreType.DMA((2, 6)), pltpu.SemaphoreType.DMA((2, 6)),
        ],
        compiler_params=pltpu.CompilerParams(
            collective_id=0, has_side_effects=True, vmem_limit_bytes=48 << 20
        ),
    )(
        latent_field, east_courant, north_courant, mixing, sunlit, decode_w, react_a, react_b,
        stoich, encode_w, rate_const.reshape(1, -1),
    )


def solution(mesh):
    placed = (
        P(None, None, "lat", "lon"),
        P(None, "lat", "lon"),
        P(None, "lat", "lon"),
        P(None, "lat", "lon"),
        P("lat", "lon"),
        P(),
        P(),
        P(),
        P(),
        P(),
        P(),
    )
    return jax.shard_map(
        on_device,
        mesh=mesh,
        in_specs=placed,
        out_specs=P(None, None, "lat", "lon"),
        check_vma=False,
    )
```

```python
import jax
import jax.numpy as jnp
from jax import lax
from jax.experimental import pallas as pl
from jax.experimental.pallas import tpu as pltpu
from jax.sharding import PartitionSpec as P

S = 32
LEV = 8
ROWS = 16
COLS = 128
BLOCK = 16
JOBS = ROWS // 2
FIRST = 11
F32 = jnp.float32
BF16 = jnp.bfloat16
MESH = pl.DeviceIdType.MESH


def dot(a, b):
    return jnp.dot(a, b, preferred_element_type=F32)


def kernel(
    x_hbm, ce_hbm, cn_hbm, mix_hbm, sun_hbm, dec_hbm, ra_hbm, rb_hbm, st_hbm, en_hbm, rc_hbm,
    out_hbm,
    X, da, db, w0, ep, em, epm, nps, nms, lower, upper, inv,
    ce, cn, mix, sun, mask, dec, ra, rb, st, en, rc, aw, bw, ew,
    packed, west, east, halo, to_north, to_south,
    row_sem, small_sem, weight_sem, out_sem, send_sem, recv_sem,
):
    n_lat, n_lon = lax.axis_size("lat"), lax.axis_size("lon")
    lat, lon = lax.axis_index("lat"), lax.axis_index("lon")
    north, south = {"lat": lax.rem(lat + 1, n_lat)}, {"lat": lax.rem(lat + n_lat - 1, n_lat)}
    right, left = {"lon": lax.rem(lon + 1, n_lon)}, {"lon": lax.rem(lon + n_lon - 1, n_lon)}

    barrier = pltpu.get_barrier_semaphore()
    for neighbour in (north, south, right, left):
        pl.semaphore_signal(barrier, inc=1, device_id=neighbour, device_id_type=MESH)

    small = [
        pltpu.make_async_copy(a, b, small_sem.at[i])
        for i, (a, b) in enumerate(((ce_hbm, ce), (cn_hbm, cn), (mix_hbm, mix), (sun_hbm, sun)))
    ]
    weights = [
        pltpu.make_async_copy(a, b, weight_sem.at[i])
        for i, (a, b) in enumerate(
            ((dec_hbm, dec), (ra_hbm, ra), (rb_hbm, rb), (st_hbm, st), (en_hbm, en), (rc_hbm, rc))
        )
    ]
    for copy in small:
        copy.start()

    def load_rows(i, carry):
        r, l = lax.rem(i // LEV + ROWS - 1, ROWS), lax.rem(i, LEV)
        pltpu.make_async_copy(x_hbm.at[:, l, r, :], X.at[0, r + 1, l], row_sem.at[r]).start()
        return carry

    lax.fori_loop(0, ROWS * LEV, load_rows, 0)
    for copy in weights:
        copy.start()

    def wait_row(r):
        pltpu.make_async_copy(da.at[0], X.at[0, r + 1], row_sem.at[r]).wait()

    for copy in small:
        copy.wait()
    lane = lax.broadcasted_iota(jnp.int32, (ROWS, COLS), 1)
    row = lax.broadcasted_iota(jnp.int32, (ROWS, COLS), 0)
    grid_row = row + lat * ROWS
    open_north, open_south = grid_row < n_lat * ROWS - 1, grid_row > 0
    for l in range(LEV):
        c, n = ce[l], cn[l]
        e_plus, e_minus = jnp.maximum(c, 0.0), jnp.minimum(c, 0.0)
        n_plus = jnp.where(open_north, jnp.maximum(n, 0.0), 0.0)
        n_minus = jnp.where(open_south, jnp.minimum(n, 0.0), 0.0)
        ep[l], em[l] = e_plus, e_minus
        epm[l] = jnp.where(lane == COLS - 1, e_plus, e_minus)
        w0[l] = 1.0 - (e_plus - e_minus) - (n_plus - n_minus)
        nps[l] = jnp.where(row == 0, 1.0, pltpu.roll(n_plus, 1, 0))
        nms[l] = jnp.where(row == ROWS - 1, 1.0, pltpu.roll(n_minus, ROWS - 1, 0))
        if l == 0:
            south_factor = n_minus[0:1]
            north_factor = n_plus[ROWS - 1 :]
            factors = [(north_factor, south_factor)]
        else:
            factors.append((n_plus[ROWS - 1 :], n_minus[0:1]))

    wait_row(ROWS - 1)
    wait_row(0)
    for l in range(LEV):
        to_north[0, l] = X[0, ROWS, l] * factors[l][0]
        to_south[0, l] = X[0, 1, l] * factors[l][1]
    pl.semaphore_wait(barrier, 4)

    def edge_copies(step):
        return (
            pltpu.make_async_remote_copy(
                src_ref=to_north.at[step], dst_ref=X.at[step, 0],
                send_sem=send_sem.at[step, 0], recv_sem=recv_sem.at[step, 0],
                device_id=north, device_id_type=MESH,
            ),
            pltpu.make_async_remote_copy(
                src_ref=to_south.at[step], dst_ref=X.at[step, ROWS + 1],
                send_sem=send_sem.at[step, 1], recv_sem=recv_sem.at[step, 1],
                device_id=south, device_id_type=MESH,
            ),
        )

    def side_copies(step, group):
        return (
            pltpu.make_async_remote_copy(
                src_ref=packed.at[step, group], dst_ref=west.at[step, group],
                send_sem=send_sem.at[step, 2 + 2 * group], recv_sem=recv_sem.at[step, 2 + 2 * group],
                device_id=right, device_id_type=MESH,
            ),
            pltpu.make_async_remote_copy(
                src_ref=packed.at[step, group], dst_ref=east.at[step, group],
                send_sem=send_sem.at[step, 3 + 2 * group], recv_sem=recv_sem.at[step, 3 + 2 * group],
                device_id=left, device_id_type=MESH,
            ),
        )

    for copy in edge_copies(0):
        copy.start()

    wide_lane = lax.broadcasted_iota(jnp.int32, (S, COLS), 1)

    def place(r):
        at = lax.rem(r + ROWS - FIRST, ROWS)
        return at // LEV, lax.rem(at, LEV)

    def pack_row(values, r, slot_step):
        group, slot = place(r)
        line = jnp.zeros((S, COLS), F32)
        for l in range(LEV):
            z = values[l] * epm[l, pl.ds(r, 1), :]
            line = jnp.where(wide_lane // 2 == l, pltpu.roll(z, 2 * l + 1, 1), line)
        line = pltpu.roll(line, 16 * slot, 1)
        packed[slot_step, group] = jnp.where(
            wide_lane // 16 == slot, line, packed[slot_step, group]
        )

    packed[...] = jnp.zeros_like(packed)

    def first_pack(i, carry):
        r = lax.rem(i + FIRST, ROWS)

        @pl.when((r > 0) & (r < ROWS - 1))
        def _():
            wait_row(r)

        pack_row([X[0, r + 1, l] for l in range(LEV)], r, 0)
        return carry

    for group in range(2):
        lax.fori_loop(group * 8, group * 8 + 8, first_pack, 0)
        for copy in side_copies(0, group):
            copy.start()

    pivot_upper = None
    for l in range(LEV):
        below = mix[l - 1] if l > 0 else None
        above = mix[l] if l < LEV - 1 else None
        pivot = 1.0
        if below is not None:
            pivot = pivot + below
        if above is not None:
            pivot = pivot + above
        if below is not None:
            pivot = pivot - below * pivot_upper
            lower[l] = below
        recip = 1.0 / pivot
        inv[l] = recip
        if above is not None:
            pivot_upper = above * recip
            upper[l] = pivot_upper
    block = lax.broadcasted_iota(jnp.int32, (1, COLS), 1) // BLOCK
    lit = jnp.zeros((1, COLS), jnp.int32)
    for b in range(COLS // BLOCK):
        lit = jnp.where(block == b, sun[0:1, b : b + 1], lit)
    mask[...] = lit
    for copy in weights:
        copy.wait()
    aw[...] = dot(dec[...], ra[...]).T.astype(BF16)
    bw[...] = dot(dec[...], rb[...]).T.astype(BF16)
    ew[...] = (dot(en[...], st[...]) * rc[...]).astype(BF16)

    def unpack(step, group):
        halo[step, group] = jnp.where(
            lax.rem(wide_lane, 2) == 0,
            pltpu.roll(east[step, group], COLS - 1, 1),
            pltpu.roll(west[step, group], 1, 1),
        )

    def transport(job, dest):
        step, turn = job // JOBS, lax.rem(job, JOBS)
        for k in range(2):
            r = lax.rem(2 * turn + FIRST + 2 * step + k, ROWS)
            group, slot = place(r)
            line = pltpu.roll(halo[step, group], lax.rem(COLS - 16 * slot, COLS), 1)
            solved = []
            for l in range(LEV):
                at = lambda ref: ref[l, pl.ds(r, 1), :]
                q = X[step, r + 1, l]
                side = pltpu.roll(line, COLS - (2 * l + 1), 1)
                from_west = jnp.where(wide_lane == 0, side, pltpu.roll(q * at(ep), 1, 1))
                from_east = jnp.where(
                    wide_lane == COLS - 1, side, pltpu.roll(q * at(em), COLS - 1, 1)
                )
                value = (
                    q * at(w0)
                    + (from_west - from_east)
                    + (X[step, r, l] * at(nps) - X[step, r + 2, l] * at(nms))
                )
                if l > 0:
                    value = value + at(lower) * solved[-1]
                solved.append(value * at(inv))
            value = solved[-1]
            dest[k, LEV - 1] = value
            for l in range(LEV - 2, -1, -1):
                value = solved[l] + upper[l, pl.ds(r, 1), :] * value
                dest[k, l] = value

    def chemistry(job, source):
        step, turn = job // JOBS, lax.rem(job, JOBS)
        current = jnp.concatenate([source[k, l] for k in range(2) for l in range(LEV)], axis=1)
        summed = None
        for substep in range(2):
            lines = current.astype(BF16)
            rates = (dot(aw[...], lines) * dot(bw[...], lines)).astype(BF16)
            change = dot(ew[...], rates)
            summed = change if summed is None else summed + change
            current = current + change
        lit_lanes = jnp.broadcast_to(mask[...], (S, COLS)) > 0
        for k in range(2):
            r = lax.rem(2 * turn + FIRST + 2 * step + k, ROWS)
            values = []
            for l in range(LEV):
                at = (k * LEV + l) * COLS
                value = source[k, l] + jnp.where(lit_lanes, summed[:, at : at + COLS], 0.0)
                X[step + 1, r + 1, l] = value
                values.append(value)
            pack_row(values, r, step + 1)

    def after(job):
        @pl.when(job == 2)
        def _():
            for l in range(LEV):
                to_north[1, l] = X[1, ROWS, l] * jnp.where(
                    lat < n_lat - 1, jnp.maximum(cn[l, ROWS - 1 :, :], 0.0), 0.0
                )
                to_south[1, l] = X[1, 1, l] * jnp.where(
                    lat > 0, jnp.minimum(cn[l, 0:1, :], 0.0), 0.0
                )
            for copy in edge_copies(1):
                copy.start()

        for group in range(2):

            @pl.when(job == 3 + 4 * group)
            def _():
                for copy in side_copies(1, group):
                    copy.start()

        @pl.when(job >= JOBS)
        def _():
            def store(i, carry):
                r = lax.rem(2 * (job - JOBS) + FIRST + 2 + i // LEV, ROWS)
                l = lax.rem(i, LEV)
                pltpu.make_async_copy(X.at[2, r + 1, l], out_hbm.at[:, l, r, :], out_sem).start()
                return carry

            lax.fori_loop(0, 2 * LEV, store, 0)

    def before(job):
        @pl.when(job == JOBS - 1)
        def _():
            for copy in edge_copies(1):
                copy.wait()
            for copy in side_copies(1, 0):
                copy.wait()
            unpack(1, 0)

        @pl.when(job == JOBS + 2)
        def _():
            for copy in side_copies(1, 1):
                copy.wait()
            unpack(1, 1)

    for copy in edge_copies(0):
        copy.wait()
    for group in range(2):
        for copy in side_copies(0, group):
            copy.wait()
        unpack(0, group)
    transport(0, da)

    def pair(i, carry):
        for k, (here, there) in enumerate(((da, db), (db, da))):
            job = 2 * i + k
            before(job)
            transport(jnp.minimum(job + 1, 2 * JOBS - 1), there)
            chemistry(job, here)
            after(job)
        return carry

    lax.fori_loop(0, JOBS, pair, 0)
    pltpu.make_async_copy(X.at[0, 1 : ROWS + 1], X.at[2, 1 : ROWS + 1], out_sem).wait()


def on_device(latent_field, east_courant, north_courant, mixing, sunlit, decode_w, react_a, react_b, stoich, encode_w, rate_const):
    coefficient = pltpu.VMEM((LEV, ROWS, COLS), F32)
    tile = pltpu.VMEM((2, LEV, S, COLS), F32)
    n_species, n_reactions = stoich.shape
    return pl.pallas_call(
        kernel,
        name="split_steps",
        out_shape=jax.ShapeDtypeStruct(latent_field.shape, F32),
        in_specs=[pl.BlockSpec(memory_space=pl.ANY)] * 11,
        out_specs=pl.BlockSpec(memory_space=pl.ANY),
        scratch_shapes=[
            pltpu.VMEM((3, ROWS + 2, LEV, S, COLS), F32), tile, tile,
            coefficient, coefficient, coefficient, coefficient, coefficient, coefficient,
            coefficient, coefficient, coefficient,
            coefficient, coefficient, pltpu.VMEM((LEV - 1, ROWS, COLS), F32),
            pltpu.VMEM((1, COLS // BLOCK), jnp.int32), pltpu.VMEM((1, COLS), jnp.int32),
            pltpu.VMEM((S, n_species), BF16),
            pltpu.VMEM((n_species, n_reactions), BF16), pltpu.VMEM((n_species, n_reactions), BF16),
            pltpu.VMEM((n_species, n_reactions), BF16), pltpu.VMEM((S, n_species), BF16),
            pltpu.VMEM((1, n_reactions), F32),
            pltpu.VMEM((n_reactions, S), BF16), pltpu.VMEM((n_reactions, S), BF16),
            pltpu.VMEM((S, n_reactions), BF16),
            pltpu.VMEM((3, 2, S, COLS), F32), pltpu.VMEM((2, 2, S, COLS), F32),
            pltpu.VMEM((2, 2, S, COLS), F32), pltpu.VMEM((2, 2, S, COLS), F32),
            pltpu.VMEM((2, LEV, S, COLS), F32), pltpu.VMEM((2, LEV, S, COLS), F32),
            pltpu.SemaphoreType.DMA((ROWS,)), pltpu.SemaphoreType.DMA((4,)),
            pltpu.SemaphoreType.DMA((6,)), pltpu.SemaphoreType.DMA,
            pltpu.SemaphoreType.DMA((2, 6)), pltpu.SemaphoreType.DMA((2, 6)),
        ],
        compiler_params=pltpu.CompilerParams(
            collective_id=0, has_side_effects=True
        ),
    )(
        latent_field, east_courant, north_courant, mixing, sunlit, decode_w.T, react_a.T,
        react_b.T, stoich, encode_w, rate_const.reshape(1, -1),
    )


def solution(mesh):
    placed = (
        P(None, None, "lat", "lon"),
        P(None, "lat", "lon"),
        P(None, "lat", "lon"),
        P(None, "lat", "lon"),
        P("lat", "lon"),
        P(),
        P(),
        P(),
        P(),
        P(),
        P(),
    )
    return jax.shard_map(
        on_device,
        mesh=mesh,
        in_specs=placed,
        out_specs=P(None, None, "lat", "lon"),
        check_vma=False,
    )
```

```python
import jax
import jax.numpy as jnp
from jax import lax
from jax.experimental import pallas as pl
from jax.experimental.pallas import tpu as pltpu
from jax.sharding import PartitionSpec as P

S = 32
LEV = 8
ROWS = 16
COLS = 128
BLOCK = 16
JOBS = ROWS // 2
FIRST = 11
F32 = jnp.float32
BF16 = jnp.bfloat16
MESH = pl.DeviceIdType.MESH


def dot(a, b):
    return jnp.dot(a, b, preferred_element_type=F32)


def dot_t(a, b):
    return lax.dot_general(a, b, (((1,), (1,)), ((), ())), preferred_element_type=F32)


def kernel(
    x_hbm, ce_hbm, cn_hbm, mix_hbm, sun_hbm, dec_hbm, ra_hbm, rb_hbm, st_hbm, en_hbm, rc_hbm,
    out,
    raw, X, da, db, edge, w0, ep, em, epm, nps, nms, lower, upper, inv,
    ce, cn, mix, sun, mask, dec, ra, rb, st, en, rc, quad, mid,
    packed, west, east, halo, to_north, to_south,
    level_sem, small_sem, weight_sem, send_sem, recv_sem,
):
    n_lat, n_lon = lax.axis_size("lat"), lax.axis_size("lon")
    lat, lon = lax.axis_index("lat"), lax.axis_index("lon")
    north, south = {"lat": lax.rem(lat + 1, n_lat)}, {"lat": lax.rem(lat + n_lat - 1, n_lat)}
    right, left = {"lon": lax.rem(lon + 1, n_lon)}, {"lon": lax.rem(lon + n_lon - 1, n_lon)}

    barrier = pltpu.get_barrier_semaphore()
    for neighbour in (north, south, right, left):
        pl.semaphore_signal(barrier, inc=1, device_id=neighbour, device_id_type=MESH)

    small = [
        pltpu.make_async_copy(a, b, small_sem.at[i])
        for i, (a, b) in enumerate(((ce_hbm, ce), (cn_hbm, cn), (mix_hbm, mix), (sun_hbm, sun)))
    ]
    weights = [
        pltpu.make_async_copy(a, b, weight_sem.at[i])
        for i, (a, b) in enumerate(
            ((dec_hbm, dec), (ra_hbm, ra), (rb_hbm, rb), (st_hbm, st), (en_hbm, en), (rc_hbm, rc))
        )
    ]
    for copy in small:
        copy.start()

    def level_copy(l):
        return pltpu.make_async_copy(x_hbm.at[:, l], raw.at[:, l], level_sem.at[l])

    for l in range(LEV):
        level_copy(l).start()
    for copy in weights:
        copy.start()

    for copy in small:
        copy.wait()
    lane = lax.broadcasted_iota(jnp.int32, (ROWS, COLS), 1)
    row = lax.broadcasted_iota(jnp.int32, (ROWS, COLS), 0)
    grid_row = row + lat * ROWS
    open_north, open_south = grid_row < n_lat * ROWS - 1, grid_row > 0
    for l in range(LEV):
        c, n = ce[l], cn[l]
        e_plus, e_minus = jnp.maximum(c, 0.0), jnp.minimum(c, 0.0)
        n_plus = jnp.where(open_north, jnp.maximum(n, 0.0), 0.0)
        n_minus = jnp.where(open_south, jnp.minimum(n, 0.0), 0.0)
        ep[l], em[l] = e_plus, e_minus
        epm[l] = jnp.where(lane == COLS - 1, e_plus, e_minus)
        w0[l] = 1.0 - (e_plus - e_minus) - (n_plus - n_minus)
        nps[l] = jnp.where(row == 0, 1.0, pltpu.roll(n_plus, 1, 0))
        nms[l] = jnp.where(row == ROWS - 1, 1.0, pltpu.roll(n_minus, ROWS - 1, 0))
        edge[l, 0:1], edge[l, 1:2] = n_plus[ROWS - 1 :], n_minus[0:1]

    def edge_copies(step):
        return (
            pltpu.make_async_remote_copy(
                src_ref=to_north.at[step], dst_ref=X.at[step, 0],
                send_sem=send_sem.at[step, 0], recv_sem=recv_sem.at[step, 0],
                device_id=north, device_id_type=MESH,
            ),
            pltpu.make_async_remote_copy(
                src_ref=to_south.at[step], dst_ref=X.at[step, ROWS + 1],
                send_sem=send_sem.at[step, 1], recv_sem=recv_sem.at[step, 1],
                device_id=south, device_id_type=MESH,
            ),
        )

    def side_copies(step, group):
        return (
            pltpu.make_async_remote_copy(
                src_ref=packed.at[step, group], dst_ref=west.at[step, group],
                send_sem=send_sem.at[step, 2 + 2 * group], recv_sem=recv_sem.at[step, 2 + 2 * group],
                device_id=right, device_id_type=MESH,
            ),
            pltpu.make_async_remote_copy(
                src_ref=packed.at[step, group], dst_ref=east.at[step, group],
                send_sem=send_sem.at[step, 3 + 2 * group], recv_sem=recv_sem.at[step, 3 + 2 * group],
                device_id=left, device_id_type=MESH,
            ),
        )

    wide_lane = lax.broadcasted_iota(jnp.int32, (S, COLS), 1)

    def place(r):
        at = lax.rem(r + ROWS - FIRST, ROWS)
        return at // LEV, lax.rem(at, LEV)

    def pack_row(values, r, slot_step):
        group, slot = place(r)
        line = jnp.zeros((S, COLS), F32)
        for l in range(LEV):
            z = values[l] * epm[l, pl.ds(r, 1), :]
            line = jnp.where(wide_lane // 2 == l, pltpu.roll(z, 2 * l + 1, 1), line)
        line = pltpu.roll(line, 16 * slot, 1)
        packed[slot_step, group] = jnp.where(
            wide_lane // 16 == slot, line, packed[slot_step, group]
        )

    packed[...] = jnp.zeros_like(packed)

    def first_level(l, carry):
        level_copy(l).wait()
        lines = [packed[0, 0], packed[0, 1]]
        for half in range(ROWS // 8):
            parts = [
                jnp.swapaxes(raw[s : s + 8, l, 8 * half : 8 * half + 8, :], 0, 1)
                for s in range(0, S, 8)
            ]
            for k in range(8):
                r = 8 * half + k
                value = jnp.concatenate([part[k] for part in parts], axis=0)
                X[0, r + 1, l] = value
                if r == 0:
                    to_south[0, l] = value * edge[l, 1:2]
                if r == ROWS - 1:
                    to_north[0, l] = value * edge[l, 0:1]
                group, slot = divmod((r + ROWS - FIRST) % ROWS, LEV)
                moved = pltpu.roll(value * epm[l, r : r + 1, :], 16 * slot + 2 * l + 1, 1)
                lines[group] = jnp.where(wide_lane // 2 == 8 * slot + l, moved, lines[group])
        packed[0, 0], packed[0, 1] = lines
        return carry

    lax.fori_loop(0, LEV, first_level, 0)
    pl.semaphore_wait(barrier, 4)
    for copy in side_copies(0, 0) + edge_copies(0) + side_copies(0, 1):
        copy.start()

    pivot_upper = None
    for l in range(LEV):
        below = mix[l - 1] if l > 0 else None
        above = mix[l] if l < LEV - 1 else None
        pivot = 1.0
        if below is not None:
            pivot = pivot + below
        if above is not None:
            pivot = pivot + above
        if below is not None:
            pivot = pivot - below * pivot_upper
            lower[l] = below
        recip = 1.0 / pivot
        inv[l] = recip
        if above is not None:
            pivot_upper = above * recip
            upper[l] = pivot_upper
    block = lax.broadcasted_iota(jnp.int32, (1, COLS), 1) // BLOCK
    lit = jnp.zeros((1, COLS), jnp.int32)
    for b in range(COLS // BLOCK):
        lit = jnp.where(block == b, sun[0:1, b : b + 1], lit)
    mask[...] = lit
    for copy in weights:
        copy.wait()
    a = dot(dec[...], ra[...])
    b = dot(dec[...], rb[...])
    e = dot(en[...], st[...]) * rc[...]
    pairs = []
    for d in range(S // 2 + 1):
        a_on = a if d == 0 else jnp.concatenate([a[d:], a[:d]], axis=0)
        b_on = b if d == 0 else jnp.concatenate([b[d:], b[:d]], axis=0)
        pairs.append(a * b_on if d in (0, S // 2) else a * b_on + a_on * b)
    pairs = jnp.concatenate(pairs, axis=0)
    pairs_top, e_top = pairs.astype(BF16), e.astype(BF16)
    pairs_rest = (pairs - pairs_top.astype(F32)).astype(BF16)
    e_rest = (e - e_top.astype(F32)).astype(BF16)
    quad[...] = (
        dot_t(e_top, pairs_top) + (dot_t(e_rest, pairs_top) + dot_t(e_top, pairs_rest))
    ).astype(BF16)

    def unpack(step, group):
        halo[step, group] = jnp.where(
            lax.rem(wide_lane, 2) == 0,
            pltpu.roll(east[step, group], COLS - 1, 1),
            pltpu.roll(west[step, group], 1, 1),
        )

    def transport(job, dest):
        step, turn = job // JOBS, lax.rem(job, JOBS)
        for k in range(2):
            r = lax.rem(2 * turn + FIRST + 2 * step + k, ROWS)
            group, slot = place(r)
            line = pltpu.roll(halo[step, group], lax.rem(COLS - 16 * slot, COLS), 1)
            solved = []
            for l in range(LEV):
                at = lambda ref: ref[l, pl.ds(r, 1), :]
                q = X[step, r + 1, l]
                side = pltpu.roll(line, COLS - (2 * l + 1), 1)
                from_west = jnp.where(wide_lane == 0, side, pltpu.roll(q * at(ep), 1, 1))
                from_east = jnp.where(
                    wide_lane == COLS - 1, side, pltpu.roll(q * at(em), COLS - 1, 1)
                )
                value = (
                    q * at(w0)
                    + (from_west - from_east)
                    + (X[step, r, l] * at(nps) - X[step, r + 2, l] * at(nms))
                )
                if l > 0:
                    value = value + at(lower) * solved[-1]
                solved.append(value * at(inv))
            value = solved[-1]
            dest[k, LEV - 1, 0:S] = value
            dest[k, LEV - 1, S:] = value
            for l in range(LEV - 2, -1, -1):
                value = solved[l] + upper[l, pl.ds(r, 1), :] * value
                dest[k, l, 0:S] = value
                dest[k, l, S:] = value

    def products(ref, k, l):
        shifted = [ref[k, l, 0 : 3 * S // 2]]
        shifted += [ref[k, l, b : b + S + 8] for b in range(1, 8)]
        lines = shifted[0][0:S].astype(BF16)
        return jnp.concatenate(
            [
                lines * shifted[d % 8][d // 8 * 8 : d // 8 * 8 + S].astype(BF16)
                for d in range(S // 2 + 1)
            ],
            axis=0,
        )

    def chemistry(step, job, source):
        turn = lax.rem(job, JOBS)
        lit_lanes = jnp.broadcast_to(mask[...], (S, COLS)) > 0
        for k in range(2):
            for l in range(0, LEV, 2):
                change = dot(
                    quad[...],
                    jnp.concatenate([products(source, k, l), products(source, k, l + 1)], axis=1),
                )
                for h in range(2):
                    value = source[k, l + h, 0:S] + change[:, h * COLS : (h + 1) * COLS]
                    mid[k, l + h, 0:S] = value
                    mid[k, l + h, S:] = value
        for k in range(2):
            r = lax.rem(2 * turn + FIRST + 2 * step + k, ROWS)
            values = []
            for l in range(0, LEV, 2):
                change = dot(
                    quad[...],
                    jnp.concatenate([products(mid, k, l), products(mid, k, l + 1)], axis=1),
                )
                for h in range(2):
                    value = jnp.where(
                        lit_lanes,
                        mid[k, l + h, 0:S] + change[:, h * COLS : (h + 1) * COLS],
                        source[k, l + h, 0:S],
                    )
                    X[step + 1, r + 1, l + h] = value
                    values.append(value)
            if step == 0:
                pack_row(values, r, 1)

    def send_edges():
        for l in range(LEV):
            to_north[1, l] = X[1, ROWS, l] * edge[l, 0:1]
            to_south[1, l] = X[1, 1, l] * edge[l, 1:2]
        for copy in edge_copies(1):
            copy.start()

    def send_sides(group):
        for copy in side_copies(1, group):
            copy.start()

    def wait_second():
        wait_edges(1)
        wait_sides(1, 0)

    def wait_edges(step):
        for copy in edge_copies(step):
            copy.wait()

    def wait_sides(step, group):
        for copy in side_copies(step, group):
            copy.wait()
        unpack(step, group)

    ahead = {
        1: lambda: wait_edges(0),
        3: lambda: wait_sides(0, 1),
        JOBS - 1: wait_second,
        JOBS + 2: lambda: wait_sides(1, 1),
    }
    behind = {2: send_edges, 3: lambda: send_sides(0), JOBS - 1: lambda: send_sides(1)}

    wait_sides(0, 0)
    transport(0, da)

    for step in range(2):

        def pair(i, carry):
            for k, (here, there) in enumerate(((da, db), (db, da))):
                job = 2 * i + k
                for at, act in ahead.items():
                    if at // JOBS == step and at % 2 == k:
                        pl.when(job == at)(act)
                transport(jnp.minimum(job + 1, 2 * JOBS - 1), there)
                chemistry(step, job, here)
                for at, act in behind.items():
                    if at // JOBS == step and at % 2 == k:
                        pl.when(job == at)(act)
            return carry

        lax.fori_loop(step * JOBS // 2, (step + 1) * JOBS // 2, pair, 0)

    def last_level(l, carry):
        for half in range(ROWS // 8):
            for s in range(0, S, 8):
                rows = X[2, 1 + 8 * half : 9 + 8 * half, l, s : s + 8, :]
                out[s : s + 8, l, 8 * half : 8 * half + 8, :] = jnp.swapaxes(rows, 0, 1)
        return carry

    lax.fori_loop(0, LEV, last_level, 0)


def on_device(latent_field, east_courant, north_courant, mixing, sunlit, decode_w, react_a, react_b, stoich, encode_w, rate_const):
    coefficient = pltpu.VMEM((LEV, ROWS, COLS), F32)
    tile = pltpu.VMEM((2, LEV, 2 * S, COLS), F32)
    n_species, n_reactions = stoich.shape
    return pl.pallas_call(
        kernel,
        name="split_steps",
        out_shape=pltpu.VMEM(latent_field.shape, F32),
        in_specs=[pl.BlockSpec(memory_space=pl.ANY)] * 11,
        out_specs=pl.BlockSpec(memory_space=pltpu.VMEM),
        scratch_shapes=[
            pltpu.VMEM((S, LEV, ROWS, COLS), F32),
            pltpu.VMEM((3, ROWS + 2, LEV, S, COLS), F32), tile, tile,
            pltpu.VMEM((LEV, 2, COLS), F32),
            coefficient, coefficient, coefficient, coefficient, coefficient, coefficient,
            coefficient, coefficient, coefficient,
            coefficient, coefficient, pltpu.VMEM((LEV - 1, ROWS, COLS), F32),
            pltpu.VMEM((1, COLS // BLOCK), jnp.int32), pltpu.VMEM((1, COLS), jnp.int32),
            pltpu.VMEM((S, n_species), BF16),
            pltpu.VMEM((n_species, n_reactions), BF16), pltpu.VMEM((n_species, n_reactions), BF16),
            pltpu.VMEM((n_species, n_reactions), BF16), pltpu.VMEM((S, n_species), BF16),
            pltpu.VMEM((1, n_reactions), F32),
            pltpu.VMEM((S, S * (S // 2 + 1)), BF16), tile,
            pltpu.VMEM((2, 2, S, COLS), F32), pltpu.VMEM((2, 2, S, COLS), F32),
            pltpu.VMEM((2, 2, S, COLS), F32), pltpu.VMEM((2, 2, S, COLS), F32),
            pltpu.VMEM((2, LEV, S, COLS), F32), pltpu.VMEM((2, LEV, S, COLS), F32),
            pltpu.SemaphoreType.DMA((LEV,)), pltpu.SemaphoreType.DMA((4,)),
            pltpu.SemaphoreType.DMA((6,)),
            pltpu.SemaphoreType.DMA((2, 6)), pltpu.SemaphoreType.DMA((2, 6)),
        ],
        compiler_params=pltpu.CompilerParams(
            collective_id=0, has_side_effects=True
        ),
    )(
        latent_field, east_courant, north_courant, mixing, sunlit, decode_w.T, react_a.T,
        react_b.T, stoich, encode_w, rate_const.reshape(1, -1),
    )


def solution(mesh):
    placed = (
        P(None, None, "lat", "lon"),
        P(None, "lat", "lon"),
        P(None, "lat", "lon"),
        P(None, "lat", "lon"),
        P("lat", "lon"),
        P(),
        P(),
        P(),
        P(),
        P(),
        P(),
    )
    return jax.shard_map(
        on_device,
        mesh=mesh,
        in_specs=placed,
        out_specs=P(None, None, "lat", "lon"),
        check_vma=False,
    )
```

```python
import jax
import jax.numpy as jnp
from jax import lax
from jax.experimental import pallas as pl
from jax.experimental.pallas import tpu as pltpu
from jax.sharding import PartitionSpec as P

S = 32
LEV = 8
ROWS = 16
COLS = 128
BLOCK = 16
JOBS = ROWS // 2
F32 = jnp.float32
BF16 = jnp.bfloat16
MESH = pl.DeviceIdType.MESH


def dot(a, b):
    return jnp.dot(a, b, preferred_element_type=F32)


def dot_t(a, b):
    return lax.dot_general(a, b, (((1,), (1,)), ((), ())), preferred_element_type=F32)


def kernel(
    x_hbm, ce_hbm, cn_hbm, mix_hbm, sun_hbm, dec_hbm, ra_hbm, rb_hbm, st_hbm, en_hbm, rc_hbm,
    out,
    raw, X, da, db, edge, w0, epw, emw, epm, nps, nms, lower, upper, inv,
    side_lower, side_upper, side_inv, side_epm,
    ce, cn, mix, sun, mask, dec, ra, rb, st, en, rc, quad, mid,
    packed, west, east, columns, sides, sides_mid, sides_out, to_north, to_south,
    level_sem, small_sem, weight_sem, send_sem, recv_sem,
):
    n_lat, n_lon = lax.axis_size("lat"), lax.axis_size("lon")
    lat, lon = lax.axis_index("lat"), lax.axis_index("lon")
    north, south = {"lat": lax.rem(lat + 1, n_lat)}, {"lat": lax.rem(lat + n_lat - 1, n_lat)}
    right, left = {"lon": lax.rem(lon + 1, n_lon)}, {"lon": lax.rem(lon + n_lon - 1, n_lon)}

    barrier = pltpu.get_barrier_semaphore()
    for neighbour in (north, south, right, left):
        pl.semaphore_signal(barrier, inc=1, device_id=neighbour, device_id_type=MESH)

    small = [
        pltpu.make_async_copy(a, b, small_sem.at[i])
        for i, (a, b) in enumerate(((ce_hbm, ce), (cn_hbm, cn), (mix_hbm, mix), (sun_hbm, sun)))
    ]
    weights = [
        pltpu.make_async_copy(a, b, weight_sem.at[i])
        for i, (a, b) in enumerate(
            ((dec_hbm, dec), (ra_hbm, ra), (rb_hbm, rb), (st_hbm, st), (en_hbm, en), (rc_hbm, rc))
        )
    ]
    for copy in small:
        copy.start()

    def level_copy(l):
        return pltpu.make_async_copy(x_hbm.at[:, l], raw.at[:, l], level_sem.at[l])

    for l in range(LEV):
        level_copy(l).start()
    for copy in weights:
        copy.start()

    for copy in small:
        copy.wait()
    lane = lax.broadcasted_iota(jnp.int32, (ROWS, COLS), 1)
    row = lax.broadcasted_iota(jnp.int32, (ROWS, COLS), 0)
    grid_row = row + lat * ROWS
    open_north, open_south = grid_row < n_lat * ROWS - 1, grid_row > 0
    for l in range(LEV):
        c, n = ce[l], cn[l]
        e_plus, e_minus = jnp.maximum(c, 0.0), jnp.minimum(c, 0.0)
        n_plus = jnp.where(open_north, jnp.maximum(n, 0.0), 0.0)
        n_minus = jnp.where(open_south, jnp.minimum(n, 0.0), 0.0)
        epw[l] = jnp.where(lane == 0, 0.0, pltpu.roll(e_plus, 1, 1))
        emw[l] = jnp.where(lane == COLS - 1, 0.0, pltpu.roll(e_minus, COLS - 1, 1))
        epm[l] = jnp.where(lane == COLS - 1, e_plus, e_minus)
        w0[l] = 1.0 - (e_plus - e_minus) - (n_plus - n_minus)
        nps[l] = jnp.where(row == 0, 1.0, pltpu.roll(n_plus, 1, 0))
        nms[l] = jnp.where(row == ROWS - 1, 1.0, pltpu.roll(n_minus, ROWS - 1, 0))
        edge[l, 0:1], edge[l, 1:2] = n_plus[ROWS - 1 :], n_minus[0:1]

    def edge_copies(step):
        return (
            pltpu.make_async_remote_copy(
                src_ref=to_north.at[step], dst_ref=X.at[step, 0],
                send_sem=send_sem.at[step, 0], recv_sem=recv_sem.at[step, 0],
                device_id=north, device_id_type=MESH,
            ),
            pltpu.make_async_remote_copy(
                src_ref=to_south.at[step], dst_ref=X.at[step, ROWS + 1],
                send_sem=send_sem.at[step, 1], recv_sem=recv_sem.at[step, 1],
                device_id=south, device_id_type=MESH,
            ),
        )

    def side_copies(step):
        return (
            pltpu.make_async_remote_copy(
                src_ref=packed.at[step], dst_ref=west.at[step],
                send_sem=send_sem.at[step, 2], recv_sem=recv_sem.at[step, 2],
                device_id=right, device_id_type=MESH,
            ),
            pltpu.make_async_remote_copy(
                src_ref=packed.at[step], dst_ref=east.at[step],
                send_sem=send_sem.at[step, 3], recv_sem=recv_sem.at[step, 3],
                device_id=left, device_id_type=MESH,
            ),
        )

    wide_lane = lax.broadcasted_iota(jnp.int32, (S, COLS), 1)
    packed[...] = jnp.zeros_like(packed)
    columns[...] = jnp.zeros_like(columns)

    def first_level(l, carry):
        level_copy(l).wait()
        group, start = l // 4, 32 * lax.rem(l, 4)
        line = packed[0, group]
        pair = wide_lane // 2 - start // 2
        for half in range(ROWS // 8):
            parts = [
                jnp.swapaxes(raw[s : s + 8, l, 8 * half : 8 * half + 8, :], 0, 1)
                for s in range(0, S, 8)
            ]
            for k in range(8):
                r = 8 * half + k
                value = jnp.concatenate([part[k] for part in parts], axis=0)
                X[0, r + 1, l] = value
                if r == 0:
                    to_south[0, l] = value * edge[l, 1:2]
                if r == ROWS - 1:
                    to_north[0, l] = value * edge[l, 0:1]
                moved = pltpu.roll(value * epm[l, r : r + 1, :], start + 2 * r + 1, 1)
                line = jnp.where(pair == r, moved, line)
        packed[0, group] = line
        return carry

    lax.fori_loop(0, LEV, first_level, 0)
    def send_first():
        pl.semaphore_wait(barrier, 4)
        for copy in side_copies(0) + edge_copies(0):
            copy.start()

    pl.when(lon > 0)(send_first)

    pivot_upper = None
    for l in range(LEV):
        below = mix[l - 1] if l > 0 else None
        above = mix[l] if l < LEV - 1 else None
        pivot = 1.0
        if below is not None:
            pivot = pivot + below
        if above is not None:
            pivot = pivot + above
        if below is not None:
            pivot = pivot - below * pivot_upper
            lower[l] = below
        recip = 1.0 / pivot
        inv[l] = recip
        if above is not None:
            pivot_upper = above * recip
            upper[l] = pivot_upper
    def side_form(rows):
        rows = pltpu.roll(rows, 1, 1, stride=2, stride_axis=0)
        return jnp.sum(jnp.where(lane // 2 == row, rows, 0.0), axis=0, keepdims=True)

    side_epm[...] = jnp.zeros_like(side_epm)
    for l in range(LEV):
        side_inv[l] = side_form(inv[l])
        if l > 0:
            side_lower[l] = side_form(lower[l])
        if l < LEV - 1:
            side_upper[l] = side_form(upper[l])
        side_epm[l // 4] = side_epm[l // 4] + pltpu.roll(side_form(epm[l]), 32 * (l % 4), 1)
    block = lax.broadcasted_iota(jnp.int32, (1, COLS), 1) // BLOCK
    lit = jnp.zeros((1, COLS), jnp.int32)
    for b in range(COLS // BLOCK):
        lit = jnp.where(block == b, sun[0:1, b : b + 1], lit)
    mask[...] = lit
    for copy in weights:
        copy.wait()
    a = dot(dec[...], ra[...])
    b = dot(dec[...], rb[...])
    e = dot(en[...], st[...]) * rc[...]
    pairs = []
    for d in range(S // 2 + 1):
        a_on = a if d == 0 else jnp.concatenate([a[d:], a[:d]], axis=0)
        b_on = b if d == 0 else jnp.concatenate([b[d:], b[:d]], axis=0)
        pairs.append(a * b_on if d in (0, S // 2) else a * b_on + a_on * b)
    pairs = jnp.concatenate(pairs, axis=0)
    pairs_top, e_top = pairs.astype(BF16), e.astype(BF16)
    pairs_rest = (pairs - pairs_top.astype(F32)).astype(BF16)
    e_rest = (e - e_top.astype(F32)).astype(BF16)
    quad[...] = (
        dot_t(e_top, pairs_top) + (dot_t(e_rest, pairs_top) + dot_t(e_top, pairs_rest))
    ).astype(BF16)

    def rows_of(job):
        return lax.rem(2 * job + 1, ROWS), lax.rem(2 * job + 2, ROWS)

    def transport(step, job, dest):
        lines = [columns[0], columns[1]]
        for k, r in enumerate(rows_of(job)):
            solved = []
            for l in range(LEV):
                at = lambda ref: ref[l, pl.ds(r, 1), :]
                q = X[step, r + 1, l]
                value = (
                    q * at(w0)
                    + (pltpu.roll(q, 1, 1) * at(epw) - pltpu.roll(q, COLS - 1, 1) * at(emw))
                    + (X[step, r, l] * at(nps) - X[step, r + 2, l] * at(nms))
                )
                if l > 0:
                    value = value + at(lower) * solved[-1]
                solved.append(value * at(inv))
            value = solved[-1]
            pair = wide_lane // 2 - r
            for l in range(LEV - 1, -1, -1):
                if l < LEV - 1:
                    value = solved[l] + upper[l, pl.ds(r, 1), :] * value
                dest[k, l, 0:S] = value
                dest[k, l, S:] = value
                start = 32 * (l % 4)
                moved = pltpu.roll(value, start + 2 * r + 1, 1)
                lines[l // 4] = jnp.where(pair == start // 2, moved, lines[l // 4])
        columns[0], columns[1] = lines

    def products(ref):
        shifted = [ref[0 : 3 * S // 2]]
        shifted += [ref[b : b + S + 8] for b in range(1, 8)]
        lines = shifted[0][0:S].astype(BF16)
        return jnp.concatenate(
            [
                lines * shifted[d % 8][d // 8 * 8 : d // 8 * 8 + S].astype(BF16)
                for d in range(S // 2 + 1)
            ],
            axis=0,
        )

    def changes(first, second):
        change = dot(quad[...], jnp.concatenate([products(first), products(second)], axis=1))
        return change[:, :COLS], change[:, COLS:]

    lit_lanes = jnp.broadcast_to(mask[...], (S, COLS)) > 0
    lit_sides = (
        jnp.broadcast_to(
            jnp.where(
                lax.rem(lax.broadcasted_iota(jnp.int32, (1, COLS), 1), 2) == 0,
                sun[0:1, COLS // BLOCK - 1 :],
                sun[0:1, 0:1],
            ),
            (S, COLS),
        )
        > 0
    )

    def chemistry(step, job, source):
        for k in range(2):
            for l in range(0, LEV, 2):
                for h, change in enumerate(changes(source.at[k, l], source.at[k, l + 1])):
                    value = source[k, l + h, 0:S] + change
                    mid[k, l + h, 0:S] = value
                    mid[k, l + h, S:] = value
        for k, r in enumerate(rows_of(job)):
            for l in range(0, LEV, 2):
                for h, change in enumerate(changes(mid.at[k, l], mid.at[k, l + 1])):
                    X[step + 1, r + 1, l + h] = jnp.where(
                        lit_lanes, mid[k, l + h, 0:S] + change, source[k, l + h, 0:S]
                    )

    def edge_columns(step):
        even = lax.rem(wide_lane, 2) == 0
        arrived = [
            jnp.where(
                even,
                -pltpu.roll(east[step, group], COLS - 1, 1),
                pltpu.roll(west[step, group], 1, 1),
            )
            for group in range(2)
        ]
        solved = []
        for l in range(LEV):
            value = pltpu.roll(arrived[l // 4], (COLS - 32 * (l % 4)) % COLS, 1)
            if l > 0:
                value = value + side_lower[l] * solved[-1]
            solved.append(value * side_inv[l])
        total = [columns[0], columns[1]]
        value = solved[-1]
        for l in range(LEV - 1, -1, -1):
            if l < LEV - 1:
                value = solved[l] + side_upper[l] * value
            total[l // 4] = total[l // 4] + pltpu.roll(value, 32 * (l % 4), 1)
        for group in range(2):
            sides[group, 0:S] = total[group]
            sides[group, S:] = total[group]
        for group, change in enumerate(changes(sides.at[0], sides.at[1])):
            value = total[group] + change
            sides_mid[group, 0:S] = value
            sides_mid[group, S:] = value
        for group, change in enumerate(changes(sides_mid.at[0], sides_mid.at[1])):
            value = jnp.where(lit_sides, sides_mid[group, 0:S] + change, total[group])
            sides_out[group] = value
            if step == 0:
                packed[1, group] = value * side_epm[group]

    edge_lane = lax.rem(lax.broadcasted_iota(jnp.int32, (8, COLS), 1) + 1, COLS) < 2

    def patched(line, values, l, r):
        shift = COLS - (32 * lax.rem(l, 4) + 2 * r + 1)
        return jnp.where(edge_lane, pltpu.roll(line, shift, 1), values)

    def patch_level(l, carry):
        for s in range(0, S, 8):
            line = sides_out[l // 4, s : s + 8]
            for r in range(ROWS):
                X[1, r + 1, l, s : s + 8] = patched(line, X[1, r + 1, l, s : s + 8], l, r)
        return carry

    def send_edges():
        for l in range(LEV):
            to_north[1, l] = X[1, ROWS, l] * edge[l, 0:1]
            to_south[1, l] = X[1, 1, l] * edge[l, 1:2]
        for copy in edge_copies(1):
            copy.start()

    for step in range(2):
        transport(step, 0, da)

        def pair(i, carry):
            transport(step, 2 * i + 1, db)
            chemistry(step, 2 * i, da)
            transport(step, 2 * i + 2, da)
            chemistry(step, 2 * i + 1, db)
            if step == 0:
                pl.when((i == 1) & (lon == 0))(send_first)
            return carry

        lax.fori_loop(0, JOBS // 2 - 1, pair, 0)
        for copy in edge_copies(step):
            copy.wait()
        transport(step, JOBS - 1, db)
        chemistry(step, JOBS - 2, da)
        for copy in side_copies(step):
            copy.wait()
        edge_columns(step)
        chemistry(step, JOBS - 1, db)
        if step == 0:
            for copy in side_copies(1):
                copy.start()
            lax.fori_loop(0, LEV, patch_level, 0)
            send_edges()

    def last_level(l, carry):
        for s in range(0, S, 8):
            line = sides_out[l // 4, s : s + 8]
            for half in range(ROWS // 8):
                rows = [
                    patched(line, X[2, 8 * half + k + 1, l, s : s + 8], l, 8 * half + k)
                    for k in range(8)
                ]
                out[s : s + 8, l, 8 * half : 8 * half + 8, :] = jnp.swapaxes(jnp.stack(rows), 0, 1)
        return carry

    lax.fori_loop(0, LEV, last_level, 0)


def on_device(latent_field, east_courant, north_courant, mixing, sunlit, decode_w, react_a, react_b, stoich, encode_w, rate_const):
    coefficient = pltpu.VMEM((LEV, ROWS, COLS), F32)
    tile = pltpu.VMEM((2, LEV, 2 * S, COLS), F32)
    side = pltpu.VMEM((LEV, 1, COLS), F32)
    n_species, n_reactions = stoich.shape
    return pl.pallas_call(
        kernel,
        name="split_steps",
        out_shape=pltpu.VMEM(latent_field.shape, F32),
        in_specs=[pl.BlockSpec(memory_space=pl.ANY)] * 11,
        out_specs=pl.BlockSpec(memory_space=pltpu.VMEM),
        scratch_shapes=[
            pltpu.VMEM((S, LEV, ROWS, COLS), F32),
            pltpu.VMEM((3, ROWS + 2, LEV, S, COLS), F32), tile, tile,
            pltpu.VMEM((LEV, 2, COLS), F32),
            coefficient, coefficient, coefficient, coefficient, coefficient, coefficient,
            coefficient, coefficient, coefficient,
            side, side, side, pltpu.VMEM((2, 1, COLS), F32),
            coefficient, coefficient, pltpu.VMEM((LEV - 1, ROWS, COLS), F32),
            pltpu.VMEM((1, COLS // BLOCK), jnp.int32), pltpu.VMEM((1, COLS), jnp.int32),
            pltpu.VMEM((S, n_species), BF16),
            pltpu.VMEM((n_species, n_reactions), BF16), pltpu.VMEM((n_species, n_reactions), BF16),
            pltpu.VMEM((n_species, n_reactions), BF16), pltpu.VMEM((S, n_species), BF16),
            pltpu.VMEM((1, n_reactions), F32),
            pltpu.VMEM((S, S * (S // 2 + 1)), BF16), tile,
            pltpu.VMEM((2, 2, S, COLS), F32), pltpu.VMEM((2, 2, S, COLS), F32),
            pltpu.VMEM((2, 2, S, COLS), F32), pltpu.VMEM((2, S, COLS), F32),
            pltpu.VMEM((2, 2 * S, COLS), F32), pltpu.VMEM((2, 2 * S, COLS), F32),
            pltpu.VMEM((2, S, COLS), F32),
            pltpu.VMEM((2, LEV, S, COLS), F32), pltpu.VMEM((2, LEV, S, COLS), F32),
            pltpu.SemaphoreType.DMA((LEV,)), pltpu.SemaphoreType.DMA((4,)),
            pltpu.SemaphoreType.DMA((6,)),
            pltpu.SemaphoreType.DMA((2, 4)), pltpu.SemaphoreType.DMA((2, 4)),
        ],
        compiler_params=pltpu.CompilerParams(
            collective_id=0, has_side_effects=True
        ),
    )(
        latent_field, east_courant, north_courant, mixing, sunlit, decode_w.T, react_a.T,
        react_b.T, stoich, encode_w, rate_const.reshape(1, -1),
    )


def solution(mesh):
    placed = (
        P(None, None, "lat", "lon"),
        P(None, "lat", "lon"),
        P(None, "lat", "lon"),
        P(None, "lat", "lon"),
        P("lat", "lon"),
        P(),
        P(),
        P(),
        P(),
        P(),
        P(),
    )
    return jax.shard_map(
        on_device,
        mesh=mesh,
        in_specs=placed,
        out_specs=P(None, None, "lat", "lon"),
        check_vma=False,
    )
```

```python
import jax
import jax.numpy as jnp
from jax import lax
from jax.experimental import pallas as pl
from jax.experimental.pallas import tpu as pltpu
from jax.sharding import PartitionSpec as P

S = 32
LEV = 8
ROWS = 16
COLS = 128
BLOCK = 16
JOBS = ROWS // 2
F32 = jnp.float32
BF16 = jnp.bfloat16
MESH = pl.DeviceIdType.MESH


def dot(a, b):
    return jnp.dot(a, b, preferred_element_type=F32)


def dot_t(a, b):
    return lax.dot_general(a, b, (((1,), (1,)), ((), ())), preferred_element_type=F32)


def patched(line, values, edge_lane, l, r):
    shift = COLS - (32 * (l % 4) + 2 * r + 1)
    return jnp.where(edge_lane, pltpu.roll(line, shift, 1), values)


def kernel(
    x_hbm, ce_hbm, cn_hbm, mix_hbm, sun_hbm, dec_hbm, ra_hbm, rb_hbm, st_hbm, en_hbm, rc_hbm,
    rows_out, sides_out,
    raw, X, da, db, edge, w0, epw, emw, epm, nps, nms, lower, upper, inv,
    side_lower, side_upper, side_inv, side_epm,
    ce, cn, mix, sun, mask, dec, ra, rb, st, en, rc, quad, mid,
    packed, west, east, columns, sides, sides_mid, to_north, to_south,
    level_sem, small_sem, weight_sem, send_sem, recv_sem,
):
    n_lat, n_lon = lax.axis_size("lat"), lax.axis_size("lon")
    lat, lon = lax.axis_index("lat"), lax.axis_index("lon")
    north, south = {"lat": lax.rem(lat + 1, n_lat)}, {"lat": lax.rem(lat + n_lat - 1, n_lat)}
    right, left = {"lon": lax.rem(lon + 1, n_lon)}, {"lon": lax.rem(lon + n_lon - 1, n_lon)}

    barrier = pltpu.get_barrier_semaphore()
    for neighbour in (north, south, right, left):
        pl.semaphore_signal(barrier, inc=1, device_id=neighbour, device_id_type=MESH)

    small = [
        pltpu.make_async_copy(a, b, small_sem.at[i])
        for i, (a, b) in enumerate(((ce_hbm, ce), (cn_hbm, cn), (mix_hbm, mix), (sun_hbm, sun)))
    ]
    weights = [
        pltpu.make_async_copy(a, b, weight_sem.at[i])
        for i, (a, b) in enumerate(
            ((dec_hbm, dec), (ra_hbm, ra), (rb_hbm, rb), (st_hbm, st), (en_hbm, en), (rc_hbm, rc))
        )
    ]
    for copy in small:
        copy.start()

    def level_copy(l):
        return pltpu.make_async_copy(x_hbm.at[:, l], raw.at[:, l], level_sem.at[l])

    for l in range(LEV):
        level_copy(l).start()
    for copy in weights:
        copy.start()

    for copy in small:
        copy.wait()
    lane = lax.broadcasted_iota(jnp.int32, (ROWS, COLS), 1)
    row = lax.broadcasted_iota(jnp.int32, (ROWS, COLS), 0)
    grid_row = row + lat * ROWS
    open_north, open_south = grid_row < n_lat * ROWS - 1, grid_row > 0
    for l in range(LEV):
        c, n = ce[l], cn[l]
        e_plus, e_minus = jnp.maximum(c, 0.0), jnp.minimum(c, 0.0)
        n_plus = jnp.where(open_north, jnp.maximum(n, 0.0), 0.0)
        n_minus = jnp.where(open_south, jnp.minimum(n, 0.0), 0.0)
        epw[l] = jnp.where(lane == 0, 0.0, pltpu.roll(e_plus, 1, 1))
        emw[l] = jnp.where(lane == COLS - 1, 0.0, pltpu.roll(e_minus, COLS - 1, 1))
        epm[l] = jnp.where(lane == COLS - 1, e_plus, e_minus)
        w0[l] = 1.0 - (e_plus - e_minus) - (n_plus - n_minus)
        nps[l] = jnp.where(row == 0, 1.0, pltpu.roll(n_plus, 1, 0))
        nms[l] = jnp.where(row == ROWS - 1, 1.0, pltpu.roll(n_minus, ROWS - 1, 0))
        edge[l, 0:1], edge[l, 1:2] = n_plus[ROWS - 1 :], n_minus[0:1]

    def edge_copies(step):
        return (
            pltpu.make_async_remote_copy(
                src_ref=to_north.at[step], dst_ref=X.at[step, 0],
                send_sem=send_sem.at[step, 0], recv_sem=recv_sem.at[step, 0],
                device_id=north, device_id_type=MESH,
            ),
            pltpu.make_async_remote_copy(
                src_ref=to_south.at[step], dst_ref=X.at[step, ROWS + 1],
                send_sem=send_sem.at[step, 1], recv_sem=recv_sem.at[step, 1],
                device_id=south, device_id_type=MESH,
            ),
        )

    def side_copies(step):
        return (
            pltpu.make_async_remote_copy(
                src_ref=packed.at[step], dst_ref=west.at[step],
                send_sem=send_sem.at[step, 2], recv_sem=recv_sem.at[step, 2],
                device_id=right, device_id_type=MESH,
            ),
            pltpu.make_async_remote_copy(
                src_ref=packed.at[step], dst_ref=east.at[step],
                send_sem=send_sem.at[step, 3], recv_sem=recv_sem.at[step, 3],
                device_id=left, device_id_type=MESH,
            ),
        )

    wide_lane = lax.broadcasted_iota(jnp.int32, (S, COLS), 1)
    packed[...] = jnp.zeros_like(packed)
    columns[...] = jnp.zeros_like(columns)

    pivot_upper = None
    for l in range(LEV):
        below = mix[l - 1] if l > 0 else None
        above = mix[l] if l < LEV - 1 else None
        pivot = 1.0
        if below is not None:
            pivot = pivot + below
        if above is not None:
            pivot = pivot + above
        if below is not None:
            pivot = pivot - below * pivot_upper
            lower[l] = below
        recip = 1.0 / pivot
        inv[l] = recip
        if above is not None:
            pivot_upper = above * recip
            upper[l] = pivot_upper
    def side_form(rows):
        rows = pltpu.roll(rows, 1, 1, stride=2, stride_axis=0)
        return jnp.sum(jnp.where(lane // 2 == row, rows, 0.0), axis=0, keepdims=True)

    side_epm[...] = jnp.zeros_like(side_epm)
    for l in range(LEV):
        side_inv[l] = side_form(inv[l])
        if l > 0:
            side_lower[l] = side_form(lower[l])
        if l < LEV - 1:
            side_upper[l] = side_form(upper[l])
        side_epm[l // 4] = side_epm[l // 4] + pltpu.roll(side_form(epm[l]), 32 * (l % 4), 1)
    def first_level(l, carry):
        level_copy(l).wait()
        group, start = l // 4, 32 * lax.rem(l, 4)
        line = packed[0, group]
        pair = wide_lane // 2 - start // 2
        for half in range(ROWS // 8):
            parts = [
                jnp.swapaxes(raw[s : s + 8, l, 8 * half : 8 * half + 8, :], 0, 1)
                for s in range(0, S, 8)
            ]
            for k in range(8):
                r = 8 * half + k
                value = jnp.concatenate([part[k] for part in parts], axis=0)
                X[0, r + 1, l] = value
                if r == 0:
                    to_south[0, l] = value * edge[l, 1:2]
                if r == ROWS - 1:
                    to_north[0, l] = value * edge[l, 0:1]
                moved = pltpu.roll(value * epm[l, r : r + 1, :], start + 2 * r + 1, 1)
                line = jnp.where(pair == r, moved, line)
        packed[0, group] = line
        return carry

    lax.fori_loop(0, LEV, first_level, 0)
    def send_first():
        pl.semaphore_wait(barrier, 4)
        for copy in side_copies(0) + edge_copies(0):
            copy.start()

    pl.when(lon > 0)(send_first)

    block = lax.broadcasted_iota(jnp.int32, (1, COLS), 1) // BLOCK
    lit = jnp.zeros((1, COLS), jnp.int32)
    for b in range(COLS // BLOCK):
        lit = jnp.where(block == b, sun[0:1, b : b + 1], lit)
    mask[...] = lit
    for copy in weights:
        copy.wait()
    a = dot(dec[...], ra[...])
    b = dot(dec[...], rb[...])
    e = dot(en[...], st[...]) * rc[...]
    pairs = []
    for d in range(S // 2 + 1):
        a_on = a if d == 0 else jnp.concatenate([a[d:], a[:d]], axis=0)
        b_on = b if d == 0 else jnp.concatenate([b[d:], b[:d]], axis=0)
        pairs.append(a * b_on if d in (0, S // 2) else a * b_on + a_on * b)
    pairs = jnp.concatenate(pairs, axis=0)
    pairs_top, e_top = pairs.astype(BF16), e.astype(BF16)
    pairs_rest = (pairs - pairs_top.astype(F32)).astype(BF16)
    e_rest = (e - e_top.astype(F32)).astype(BF16)
    quad[...] = (
        dot_t(e_top, pairs_top) + (dot_t(e_rest, pairs_top) + dot_t(e_top, pairs_rest))
    ).astype(BF16)

    def rows_of(job):
        return lax.rem(2 * job + 1, ROWS), lax.rem(2 * job + 2, ROWS)

    def transport(step, job, dest):
        lines = [columns[0], columns[1]]
        for k, r in enumerate(rows_of(job)):
            solved = []
            for l in range(LEV):
                at = lambda ref: ref[l, pl.ds(r, 1), :]
                q = X[step, r + 1, l]
                value = (
                    q * at(w0)
                    + (pltpu.roll(q, 1, 1) * at(epw) - pltpu.roll(q, COLS - 1, 1) * at(emw))
                    + (X[step, r, l] * at(nps) - X[step, r + 2, l] * at(nms))
                )
                if l > 0:
                    value = value + at(lower) * solved[-1]
                solved.append(value * at(inv))
            value = solved[-1]
            pair = wide_lane // 2 - r
            for l in range(LEV - 1, -1, -1):
                if l < LEV - 1:
                    value = solved[l] + upper[l, pl.ds(r, 1), :] * value
                dest[k, l, 0:S] = value
                dest[k, l, S:] = value
                start = 32 * (l % 4)
                moved = pltpu.roll(value, start + 2 * r + 1, 1)
                lines[l // 4] = jnp.where(pair == start // 2, moved, lines[l // 4])
        columns[0], columns[1] = lines

    def products(ref):
        shifted = [ref[0 : 3 * S // 2]]
        shifted += [ref[b : b + S + 8] for b in range(1, 8)]
        lines = shifted[0][0:S].astype(BF16)
        return jnp.concatenate(
            [
                lines * shifted[d % 8][d // 8 * 8 : d // 8 * 8 + S].astype(BF16)
                for d in range(S // 2 + 1)
            ],
            axis=0,
        )

    def changes(first, second):
        change = dot(quad[...], jnp.concatenate([products(first), products(second)], axis=1))
        return change[:, :COLS], change[:, COLS:]

    lit_lanes = jnp.broadcast_to(mask[...], (S, COLS)) > 0
    lit_sides = (
        jnp.broadcast_to(
            jnp.where(
                lax.rem(lax.broadcasted_iota(jnp.int32, (1, COLS), 1), 2) == 0,
                sun[0:1, COLS // BLOCK - 1 :],
                sun[0:1, 0:1],
            ),
            (S, COLS),
        )
        > 0
    )

    def chemistry(step, job, source):
        for k in range(2):
            for l in range(0, LEV, 2):
                for h, change in enumerate(changes(source.at[k, l], source.at[k, l + 1])):
                    value = source[k, l + h, 0:S] + change
                    mid[k, l + h, 0:S] = value
                    mid[k, l + h, S:] = value
        for k, r in enumerate(rows_of(job)):
            for l in range(0, LEV, 2):
                for h, change in enumerate(changes(mid.at[k, l], mid.at[k, l + 1])):
                    value = jnp.where(
                        lit_lanes, mid[k, l + h, 0:S] + change, source[k, l + h, 0:S]
                    )
                    if step == 0:
                        X[1, r + 1, l + h] = value
                    else:
                        rows_out[r, l + h] = value

    def edge_columns(step):
        even = lax.rem(wide_lane, 2) == 0
        arrived = [
            jnp.where(
                even,
                -pltpu.roll(east[step, group], COLS - 1, 1),
                pltpu.roll(west[step, group], 1, 1),
            )
            for group in range(2)
        ]
        solved = []
        for l in range(LEV):
            value = pltpu.roll(arrived[l // 4], (COLS - 32 * (l % 4)) % COLS, 1)
            if l > 0:
                value = value + side_lower[l] * solved[-1]
            solved.append(value * side_inv[l])
        total = [columns[0], columns[1]]
        value = solved[-1]
        for l in range(LEV - 1, -1, -1):
            if l < LEV - 1:
                value = solved[l] + side_upper[l] * value
            total[l // 4] = total[l // 4] + pltpu.roll(value, 32 * (l % 4), 1)
        for group in range(2):
            sides[group, 0:S] = total[group]
            sides[group, S:] = total[group]
        for group, change in enumerate(changes(sides.at[0], sides.at[1])):
            value = total[group] + change
            sides_mid[group, 0:S] = value
            sides_mid[group, S:] = value
        for group, change in enumerate(changes(sides_mid.at[0], sides_mid.at[1])):
            value = jnp.where(lit_sides, sides_mid[group, 0:S] + change, total[group])
            sides_out[group] = value
            if step == 0:
                packed[1, group] = value * side_epm[group]

    edge_lane = lax.rem(lax.broadcasted_iota(jnp.int32, (8, COLS), 1) + 1, COLS) < 2

    def patch_level(l, carry):
        for s in range(0, S, 8):
            line = sides_out[l // 4, s : s + 8]
            for r in range(ROWS):
                X[1, r + 1, l, s : s + 8] = patched(
                    line, X[1, r + 1, l, s : s + 8], edge_lane, l, r
                )
        return carry

    def send_edges():
        for l in range(LEV):
            to_north[1, l] = X[1, ROWS, l] * edge[l, 0:1]
            to_south[1, l] = X[1, 1, l] * edge[l, 1:2]
        for copy in edge_copies(1):
            copy.start()

    for step in range(2):
        transport(step, 0, da)

        def pair(i, carry):
            transport(step, 2 * i + 1, db)
            chemistry(step, 2 * i, da)
            transport(step, 2 * i + 2, da)
            chemistry(step, 2 * i + 1, db)
            if step == 0:
                pl.when((i == 0) & (lon == 0))(send_first)
            return carry

        lax.fori_loop(0, JOBS // 2 - 1, pair, 0)
        for copy in edge_copies(step):
            copy.wait()
        transport(step, JOBS - 1, db)
        chemistry(step, JOBS - 2, da)
        for copy in side_copies(step):
            copy.wait()
        edge_columns(step)
        chemistry(step, JOBS - 1, db)
        if step == 0:
            for copy in side_copies(1):
                copy.start()
            lax.fori_loop(0, LEV, patch_level, 0)
            send_edges()


def finish(rows_in, sides_out, out, whole, sem):
    edge_lane = lax.rem(lax.broadcasted_iota(jnp.int32, (8, COLS), 1) + 1, COLS) < 2

    def level_copy(l):
        return pltpu.make_async_copy(whole.at[:, l], out.at[:, l], sem.at[l])

    for l in range(LEV):
        for s in range(0, S, 8):
            line = sides_out[l // 4, s : s + 8]
            for half in range(ROWS // 8):
                rows = [
                    patched(line, rows_in[r, l, s : s + 8], edge_lane, l, r)
                    for r in range(8 * half, 8 * half + 8)
                ]
                whole[s : s + 8, l, 8 * half : 8 * half + 8, :] = jnp.swapaxes(
                    jnp.stack(rows), 0, 1
                )
        level_copy(l).start()
    for l in range(LEV):
        level_copy(l).wait()


def on_device(latent_field, east_courant, north_courant, mixing, sunlit, decode_w, react_a, react_b, stoich, encode_w, rate_const):
    coefficient = pltpu.VMEM((LEV, ROWS, COLS), F32)
    tile = pltpu.VMEM((2, LEV, 2 * S, COLS), F32)
    side = pltpu.VMEM((LEV, 1, COLS), F32)
    n_species, n_reactions = stoich.shape
    rows, sides = pl.pallas_call(
        kernel,
        name="split_steps",
        out_shape=(pltpu.VMEM((ROWS, LEV, S, COLS), F32), pltpu.VMEM((2, S, COLS), F32)),
        in_specs=[pl.BlockSpec(memory_space=pl.ANY)] * 11,
        out_specs=[pl.BlockSpec(memory_space=pltpu.VMEM)] * 2,
        scratch_shapes=[
            pltpu.VMEM((S, LEV, ROWS, COLS), F32),
            pltpu.VMEM((2, ROWS + 2, LEV, S, COLS), F32), tile, tile,
            pltpu.VMEM((LEV, 2, COLS), F32),
            coefficient, coefficient, coefficient, coefficient, coefficient, coefficient,
            coefficient, coefficient, coefficient,
            side, side, side, pltpu.VMEM((2, 1, COLS), F32),
            coefficient, coefficient, pltpu.VMEM((LEV - 1, ROWS, COLS), F32),
            pltpu.VMEM((1, COLS // BLOCK), jnp.int32), pltpu.VMEM((1, COLS), jnp.int32),
            pltpu.VMEM((S, n_species), BF16),
            pltpu.VMEM((n_species, n_reactions), BF16), pltpu.VMEM((n_species, n_reactions), BF16),
            pltpu.VMEM((n_species, n_reactions), BF16), pltpu.VMEM((S, n_species), BF16),
            pltpu.VMEM((1, n_reactions), F32),
            pltpu.VMEM((S, S * (S // 2 + 1)), BF16), tile,
            pltpu.VMEM((2, 2, S, COLS), F32), pltpu.VMEM((2, 2, S, COLS), F32),
            pltpu.VMEM((2, 2, S, COLS), F32), pltpu.VMEM((2, S, COLS), F32),
            pltpu.VMEM((2, 2 * S, COLS), F32), pltpu.VMEM((2, 2 * S, COLS), F32),
            pltpu.VMEM((2, LEV, S, COLS), F32), pltpu.VMEM((2, LEV, S, COLS), F32),
            pltpu.SemaphoreType.DMA((LEV,)), pltpu.SemaphoreType.DMA((4,)),
            pltpu.SemaphoreType.DMA((6,)),
            pltpu.SemaphoreType.DMA((2, 4)), pltpu.SemaphoreType.DMA((2, 4)),
        ],
        compiler_params=pltpu.CompilerParams(
            collective_id=0, has_side_effects=True
        ),
    )(
        latent_field, east_courant, north_courant, mixing, sunlit, decode_w.T, react_a.T,
        react_b.T, stoich, encode_w, rate_const.reshape(1, -1),
    )
    return pl.pallas_call(
        finish,
        name="finish",
        out_shape=jax.ShapeDtypeStruct(latent_field.shape, F32),
        in_specs=[pl.BlockSpec(memory_space=pltpu.VMEM)] * 2,
        out_specs=pl.BlockSpec(memory_space=pl.ANY),
        scratch_shapes=[pltpu.VMEM((S, LEV, ROWS, COLS), F32), pltpu.SemaphoreType.DMA((LEV,))],
        compiler_params=pltpu.CompilerParams(vmem_limit_bytes=24 << 20),
    )(rows, sides)


def solution(mesh):
    placed = (
        P(None, None, "lat", "lon"),
        P(None, "lat", "lon"),
        P(None, "lat", "lon"),
        P(None, "lat", "lon"),
        P("lat", "lon"),
        P(),
        P(),
        P(),
        P(),
        P(),
        P(),
    )
    return jax.shard_map(
        on_device,
        mesh=mesh,
        in_specs=placed,
        out_specs=P(None, None, "lat", "lon"),
        check_vma=False,
    )
```

```python
import jax
import jax.numpy as jnp
from jax import lax
from jax.experimental import pallas as pl
from jax.experimental.pallas import tpu as pltpu
from jax.sharding import PartitionSpec as P

S = 32
LEV = 8
ROWS = 16
COLS = 128
BLOCK = 16
JOBS = ROWS // 2
F32 = jnp.float32
BF16 = jnp.bfloat16
MESH = pl.DeviceIdType.MESH


def dot(a, b):
    return jnp.dot(a, b, preferred_element_type=F32)


def dot_t(a, b):
    return lax.dot_general(a, b, (((1,), (1,)), ((), ())), preferred_element_type=F32)


def patched(line, values, edge_lane, l, r):
    shift = COLS - (32 * (l % 4) + 2 * r + 1)
    return jnp.where(edge_lane, pltpu.roll(line, shift, 1), values)


def kernel(
    x_hbm, ce_hbm, cn_hbm, mix_hbm, sun_hbm, dec_hbm, ra_hbm, rb_hbm, st_hbm, en_hbm, rc_hbm,
    rows_out, sides_out,
    raw, X, da, db, edge, w0, epw, emw, epm, nps, nms, lower, upper, inv,
    side_lower, side_upper, side_inv, side_epm,
    ce, cn, mix, sun, mask, dec, ra, rb, st, en, rc, quad, mid,
    packed, west, east, columns, sides, sides_mid, to_north, to_south,
    level_sem, small_sem, weight_sem, send_sem, recv_sem,
):
    n_lat, n_lon = lax.axis_size("lat"), lax.axis_size("lon")
    lat, lon = lax.axis_index("lat"), lax.axis_index("lon")
    north, south = {"lat": lax.rem(lat + 1, n_lat)}, {"lat": lax.rem(lat + n_lat - 1, n_lat)}
    right, left = {"lon": lax.rem(lon + 1, n_lon)}, {"lon": lax.rem(lon + n_lon - 1, n_lon)}

    small = [
        pltpu.make_async_copy(a, b, small_sem.at[i])
        for i, (a, b) in enumerate(((ce_hbm, ce), (cn_hbm, cn), (mix_hbm, mix), (sun_hbm, sun)))
    ]
    weights = [
        pltpu.make_async_copy(a, b, weight_sem.at[i])
        for i, (a, b) in enumerate(
            ((dec_hbm, dec), (ra_hbm, ra), (rb_hbm, rb), (st_hbm, st), (en_hbm, en), (rc_hbm, rc))
        )
    ]
    for copy in small:
        copy.start()

    def level_copy(l):
        return pltpu.make_async_copy(x_hbm.at[:, l], raw.at[:, l], level_sem.at[l])

    for l in range(LEV):
        level_copy(l).start()
    barrier = pltpu.get_barrier_semaphore()
    enter = lambda where: pl.semaphore_signal(
        barrier, inc=1, device_id=where, device_id_type=MESH
    )
    enter(north)
    enter(south)
    enter(left)

    for copy in weights:
        copy.start()

    for copy in small:
        copy.wait()
    lane = lax.broadcasted_iota(jnp.int32, (ROWS, COLS), 1)
    row = lax.broadcasted_iota(jnp.int32, (ROWS, COLS), 0)
    grid_row = row + lat * ROWS
    open_north, open_south = grid_row < n_lat * ROWS - 1, grid_row > 0
    for l in range(LEV):
        c, n = ce[l], cn[l]
        e_plus, e_minus = jnp.maximum(c, 0.0), jnp.minimum(c, 0.0)
        n_plus = jnp.where(open_north, jnp.maximum(n, 0.0), 0.0)
        n_minus = jnp.where(open_south, jnp.minimum(n, 0.0), 0.0)
        epw[l] = jnp.where(lane == 0, 0.0, pltpu.roll(e_plus, 1, 1))
        emw[l] = jnp.where(lane == COLS - 1, 0.0, pltpu.roll(e_minus, COLS - 1, 1))
        epm[l] = jnp.where(lane == COLS - 1, e_plus, e_minus)
        w0[l] = 1.0 - (e_plus - e_minus) - (n_plus - n_minus)
        nps[l] = jnp.where(row == 0, 1.0, pltpu.roll(n_plus, 1, 0))
        nms[l] = jnp.where(row == ROWS - 1, 1.0, pltpu.roll(n_minus, ROWS - 1, 0))
        edge[l, 0:1], edge[l, 1:2] = n_plus[ROWS - 1 :], n_minus[0:1]

    def edge_copies(step):
        return (
            pltpu.make_async_remote_copy(
                src_ref=to_north.at[step], dst_ref=X.at[step, 0],
                send_sem=send_sem.at[step, 0], recv_sem=recv_sem.at[step, 0],
                device_id=north, device_id_type=MESH,
            ),
            pltpu.make_async_remote_copy(
                src_ref=to_south.at[step], dst_ref=X.at[step, ROWS + 1],
                send_sem=send_sem.at[step, 1], recv_sem=recv_sem.at[step, 1],
                device_id=south, device_id_type=MESH,
            ),
        )

    def side_copies(step):
        return (
            pltpu.make_async_remote_copy(
                src_ref=packed.at[step], dst_ref=west.at[step],
                send_sem=send_sem.at[step, 2], recv_sem=recv_sem.at[step, 2],
                device_id=right, device_id_type=MESH,
            ),
            pltpu.make_async_remote_copy(
                src_ref=packed.at[step], dst_ref=east.at[step],
                send_sem=send_sem.at[step, 3], recv_sem=recv_sem.at[step, 3],
                device_id=left, device_id_type=MESH,
            ),
        )

    wide_lane = lax.broadcasted_iota(jnp.int32, (S, COLS), 1)
    packed[...] = jnp.zeros_like(packed)
    columns[...] = jnp.zeros_like(columns)

    pivot_upper = None
    for l in range(LEV):
        below = mix[l - 1] if l > 0 else None
        above = mix[l] if l < LEV - 1 else None
        pivot = 1.0
        if below is not None:
            pivot = pivot + below
        if above is not None:
            pivot = pivot + above
        if below is not None:
            pivot = pivot - below * pivot_upper
            lower[l] = below
        recip = 1.0 / pivot
        inv[l] = recip
        if above is not None:
            pivot_upper = above * recip
            upper[l] = pivot_upper
    def side_form(rows):
        rows = pltpu.roll(rows, 1, 1, stride=2, stride_axis=0)
        return jnp.sum(jnp.where(lane // 2 == row, rows, 0.0), axis=0, keepdims=True)

    side_epm[...] = jnp.zeros_like(side_epm)
    for l in range(LEV):
        side_inv[l] = side_form(inv[l])
        if l > 0:
            side_lower[l] = side_form(lower[l])
        if l < LEV - 1:
            side_upper[l] = side_form(upper[l])
        side_epm[l // 4] = side_epm[l // 4] + pltpu.roll(side_form(epm[l]), 32 * (l % 4), 1)
    def first_level(l, carry):
        level_copy(l).wait()
        group, start = l // 4, 32 * lax.rem(l, 4)
        line = packed[0, group]
        pair = wide_lane // 2 - start // 2
        for half in range(ROWS // 8):
            parts = [
                jnp.swapaxes(raw[s : s + 8, l, 8 * half : 8 * half + 8, :], 0, 1)
                for s in range(0, S, 8)
            ]
            for k in range(8):
                r = 8 * half + k
                value = jnp.concatenate([part[k] for part in parts], axis=0)
                X[0, r + 1, l] = value
                if r == 0:
                    to_south[0, l] = value * edge[l, 1:2]
                if r == ROWS - 1:
                    to_north[0, l] = value * edge[l, 0:1]
                moved = pltpu.roll(value * epm[l, r : r + 1, :], start + 2 * r + 1, 1)
                line = jnp.where(pair == r, moved, line)
        packed[0, group] = line
        return carry

    lax.fori_loop(0, LEV, first_level, 0)
    def start(copies):
        for copy in copies:
            copy.start()

    def arrive(copies):
        for copy in copies:
            copy.wait_recv()

    def send_first():
        pl.semaphore_wait(barrier, 3)
        start(side_copies(0)[:1] + edge_copies(0))

    def send_left_first():
        arrive(side_copies(0)[:1])
        start(side_copies(0)[1:])

    send_first()

    block = lax.broadcasted_iota(jnp.int32, (1, COLS), 1) // BLOCK
    lit = jnp.zeros((1, COLS), jnp.int32)
    for b in range(COLS // BLOCK):
        lit = jnp.where(block == b, sun[0:1, b : b + 1], lit)
    mask[...] = lit
    for copy in weights:
        copy.wait()
    a = dot(dec[...], ra[...])
    b = dot(dec[...], rb[...])
    e = dot(en[...], st[...]) * rc[...]
    pairs = []
    for d in range(S // 2 + 1):
        a_on = a if d == 0 else jnp.concatenate([a[d:], a[:d]], axis=0)
        b_on = b if d == 0 else jnp.concatenate([b[d:], b[:d]], axis=0)
        pairs.append(a * b_on if d in (0, S // 2) else a * b_on + a_on * b)
    pairs = jnp.concatenate(pairs, axis=0)
    pairs_top, e_top = pairs.astype(BF16), e.astype(BF16)
    pairs_rest = (pairs - pairs_top.astype(F32)).astype(BF16)
    e_rest = (e - e_top.astype(F32)).astype(BF16)
    quad[...] = (
        dot_t(e_top, pairs_top) + (dot_t(e_rest, pairs_top) + dot_t(e_top, pairs_rest))
    ).astype(BF16)

    def rows_of(job):
        return lax.rem(2 * job + 1, ROWS), lax.rem(2 * job + 2, ROWS)

    def transport(step, job, dest):
        lines = [columns[0], columns[1]]
        for k, r in enumerate(rows_of(job)):
            solved = []
            for l in range(LEV):
                at = lambda ref: ref[l, pl.ds(r, 1), :]
                q = X[step, r + 1, l]
                value = (
                    q * at(w0)
                    + (pltpu.roll(q, 1, 1) * at(epw) - pltpu.roll(q, COLS - 1, 1) * at(emw))
                    + (X[step, r, l] * at(nps) - X[step, r + 2, l] * at(nms))
                )
                if l > 0:
                    value = value + at(lower) * solved[-1]
                solved.append(value * at(inv))
            value = solved[-1]
            pair = wide_lane // 2 - r
            for l in range(LEV - 1, -1, -1):
                if l < LEV - 1:
                    value = solved[l] + upper[l, pl.ds(r, 1), :] * value
                dest[k, l, 0:S] = value
                dest[k, l, S:] = value
                start = 32 * (l % 4)
                moved = pltpu.roll(value, start + 2 * r + 1, 1)
                lines[l // 4] = jnp.where(pair == start // 2, moved, lines[l // 4])
        columns[0], columns[1] = lines

    def products(ref):
        shifted = [ref[0 : 3 * S // 2]]
        shifted += [ref[b : b + S + 8] for b in range(1, 8)]
        lines = shifted[0][0:S].astype(BF16)
        return jnp.concatenate(
            [
                lines * shifted[d % 8][d // 8 * 8 : d // 8 * 8 + S].astype(BF16)
                for d in range(S // 2 + 1)
            ],
            axis=0,
        )

    def changes(first, second):
        change = dot(quad[...], jnp.concatenate([products(first), products(second)], axis=1))
        return change[:, :COLS], change[:, COLS:]

    lit_lanes = jnp.broadcast_to(mask[...], (S, COLS)) > 0
    lit_sides = (
        jnp.broadcast_to(
            jnp.where(
                lax.rem(lax.broadcasted_iota(jnp.int32, (1, COLS), 1), 2) == 0,
                sun[0:1, COLS // BLOCK - 1 :],
                sun[0:1, 0:1],
            ),
            (S, COLS),
        )
        > 0
    )

    def chemistry(step, job, source):
        for k in range(2):
            for l in range(0, LEV, 2):
                for h, change in enumerate(changes(source.at[k, l], source.at[k, l + 1])):
                    value = source[k, l + h, 0:S] + change
                    mid[k, l + h, 0:S] = value
                    mid[k, l + h, S:] = value
        for k, r in enumerate(rows_of(job)):
            for l in range(0, LEV, 2):
                for h, change in enumerate(changes(mid.at[k, l], mid.at[k, l + 1])):
                    value = jnp.where(
                        lit_lanes, mid[k, l + h, 0:S] + change, source[k, l + h, 0:S]
                    )
                    if step == 0:
                        X[1, r + 1, l + h] = value
                    else:
                        rows_out[r, l + h] = value

    def edge_columns(step):
        even = lax.rem(wide_lane, 2) == 0
        arrived = [
            jnp.where(
                even,
                -pltpu.roll(east[step, group], COLS - 1, 1),
                pltpu.roll(west[step, group], 1, 1),
            )
            for group in range(2)
        ]
        solved = []
        for l in range(LEV):
            value = pltpu.roll(arrived[l // 4], (COLS - 32 * (l % 4)) % COLS, 1)
            if l > 0:
                value = value + side_lower[l] * solved[-1]
            solved.append(value * side_inv[l])
        total = [columns[0], columns[1]]
        value = solved[-1]
        for l in range(LEV - 1, -1, -1):
            if l < LEV - 1:
                value = solved[l] + side_upper[l] * value
            total[l // 4] = total[l // 4] + pltpu.roll(value, 32 * (l % 4), 1)
        for group in range(2):
            sides[group, 0:S] = total[group]
            sides[group, S:] = total[group]
        for group, change in enumerate(changes(sides.at[0], sides.at[1])):
            value = total[group] + change
            sides_mid[group, 0:S] = value
            sides_mid[group, S:] = value
        for group, change in enumerate(changes(sides_mid.at[0], sides_mid.at[1])):
            value = jnp.where(lit_sides, sides_mid[group, 0:S] + change, total[group])
            sides_out[group] = value
            if step == 0:
                packed[1, group] = value * side_epm[group]

    edge_lane = lax.rem(lax.broadcasted_iota(jnp.int32, (8, COLS), 1) + 1, COLS) < 2

    def patch_level(l, carry):
        for s in range(0, S, 8):
            line = sides_out[l // 4, s : s + 8]
            for r in range(ROWS):
                X[1, r + 1, l, s : s + 8] = patched(
                    line, X[1, r + 1, l, s : s + 8], edge_lane, l, r
                )
        return carry

    def send_edges():
        for l in range(LEV):
            to_north[1, l] = X[1, ROWS, l] * edge[l, 0:1]
            to_south[1, l] = X[1, 1, l] * edge[l, 1:2]
        for copy in edge_copies(1):
            copy.start()

    for step in range(2):
        transport(step, 0, da)

        def pair(i, carry):
            transport(step, 2 * i + 1, db)
            chemistry(step, 2 * i, da)
            transport(step, 2 * i + 2, da)
            chemistry(step, 2 * i + 1, db)
            if step == 0:
                pl.when((i == 1) & (lon > 0))(send_left_first)
            return carry

        lax.fori_loop(0, JOBS // 2 - 1, pair, 0)
        for copy in edge_copies(step):
            copy.wait()
        transport(step, JOBS - 1, db)
        chemistry(step, JOBS - 2, da)
        early = lon == 0 if step == 0 else (lon == 0) | (lon == n_lon - 1)

        @pl.when(jnp.logical_not(early))
        def _():
            arrive(side_copies(step)[1 - step :])
            edge_columns(step)
            chemistry(step, JOBS - 1, db)

        @pl.when(early)
        def _():
            chemistry(step, JOBS - 1, db)
            if step == 0:
                send_left_first()
            arrive(side_copies(step)[1 - step :])
            edge_columns(step)

        if step == 0:
            start(side_copies(1))
            lax.fori_loop(0, LEV, patch_level, 0)
            send_edges()
        for copy in side_copies(step):
            copy.wait_send()


def finish(rows_in, sides_out, out, whole, sem):
    edge_lane = lax.rem(lax.broadcasted_iota(jnp.int32, (8, COLS), 1) + 1, COLS) < 2

    def level_copy(l):
        return pltpu.make_async_copy(whole.at[:, l], out.at[:, l], sem.at[l])

    for l in range(LEV):
        for s in range(0, S, 8):
            line = sides_out[l // 4, s : s + 8]
            for half in range(ROWS // 8):
                rows = [
                    patched(line, rows_in[r, l, s : s + 8], edge_lane, l, r)
                    for r in range(8 * half, 8 * half + 8)
                ]
                whole[s : s + 8, l, 8 * half : 8 * half + 8, :] = jnp.swapaxes(
                    jnp.stack(rows), 0, 1
                )
        level_copy(l).start()
    for l in range(LEV):
        level_copy(l).wait()


def on_device(latent_field, east_courant, north_courant, mixing, sunlit, decode_w, react_a, react_b, stoich, encode_w, rate_const):
    coefficient = pltpu.VMEM((LEV, ROWS, COLS), F32)
    tile = pltpu.VMEM((2, LEV, 2 * S, COLS), F32)
    side = pltpu.VMEM((LEV, 1, COLS), F32)
    n_species, n_reactions = stoich.shape
    rows, sides = pl.pallas_call(
        kernel,
        name="split_steps",
        out_shape=(pltpu.VMEM((ROWS, LEV, S, COLS), F32), pltpu.VMEM((2, S, COLS), F32)),
        in_specs=[pl.BlockSpec(memory_space=pl.ANY)] * 11,
        out_specs=[pl.BlockSpec(memory_space=pltpu.VMEM)] * 2,
        scratch_shapes=[
            pltpu.VMEM((S, LEV, ROWS, COLS), F32),
            pltpu.VMEM((2, ROWS + 2, LEV, S, COLS), F32), tile, tile,
            pltpu.VMEM((LEV, 2, COLS), F32),
            coefficient, coefficient, coefficient, coefficient, coefficient, coefficient,
            coefficient, coefficient, coefficient,
            side, side, side, pltpu.VMEM((2, 1, COLS), F32),
            coefficient, coefficient, pltpu.VMEM((LEV - 1, ROWS, COLS), F32),
            pltpu.VMEM((1, COLS // BLOCK), jnp.int32), pltpu.VMEM((1, COLS), jnp.int32),
            pltpu.VMEM((S, n_species), BF16),
            pltpu.VMEM((n_species, n_reactions), BF16), pltpu.VMEM((n_species, n_reactions), BF16),
            pltpu.VMEM((n_species, n_reactions), BF16), pltpu.VMEM((S, n_species), BF16),
            pltpu.VMEM((1, n_reactions), F32),
            pltpu.VMEM((S, S * (S // 2 + 1)), BF16), tile,
            pltpu.VMEM((2, 2, S, COLS), F32), pltpu.VMEM((2, 2, S, COLS), F32),
            pltpu.VMEM((2, 2, S, COLS), F32), pltpu.VMEM((2, S, COLS), F32),
            pltpu.VMEM((2, 2 * S, COLS), F32), pltpu.VMEM((2, 2 * S, COLS), F32),
            pltpu.VMEM((2, LEV, S, COLS), F32), pltpu.VMEM((2, LEV, S, COLS), F32),
            pltpu.SemaphoreType.DMA((LEV,)), pltpu.SemaphoreType.DMA((4,)),
            pltpu.SemaphoreType.DMA((6,)),
            pltpu.SemaphoreType.DMA((2, 4)), pltpu.SemaphoreType.DMA((2, 4)),
        ],
        compiler_params=pltpu.CompilerParams(
            collective_id=0, has_side_effects=True
        ),
    )(
        latent_field, east_courant, north_courant, mixing, sunlit, decode_w.T, react_a.T,
        react_b.T, stoich, encode_w, rate_const.reshape(1, -1),
    )
    return pl.pallas_call(
        finish,
        name="finish",
        out_shape=jax.ShapeDtypeStruct(latent_field.shape, F32),
        in_specs=[pl.BlockSpec(memory_space=pltpu.VMEM)] * 2,
        out_specs=pl.BlockSpec(memory_space=pl.ANY),
        scratch_shapes=[pltpu.VMEM((S, LEV, ROWS, COLS), F32), pltpu.SemaphoreType.DMA((LEV,))],
        compiler_params=pltpu.CompilerParams(vmem_limit_bytes=24 << 20),
    )(rows, sides)


def solution(mesh):
    placed = (
        P(None, None, "lat", "lon"),
        P(None, "lat", "lon"),
        P(None, "lat", "lon"),
        P(None, "lat", "lon"),
        P("lat", "lon"),
        P(),
        P(),
        P(),
        P(),
        P(),
        P(),
    )
    return jax.shard_map(
        on_device,
        mesh=mesh,
        in_specs=placed,
        out_specs=P(None, None, "lat", "lon"),
        check_vma=False,
    )
```
